256 devices in a mesh: dp: 8 (over y, core), expert: 32 (over x, z).
Axes of the slice: x: 4, y: 4, z: 8, core: 2. Of those that a mesh axis runs over, the one named last changes fastest.
Arguments:
- tokens: bfloat16 [32768, 2048], P(('dp', 'expert')), may hold values from -6 to 6
- routes: int32 [32768, 4], P(('dp', 'expert')), may hold values from 0 to 31, all different within a row; in each aligned block of 128 rows (0 to 127, 128 to 255, ...) at most 24 rows name the same one
- combine: float32 [32768, 4], P(('dp', 'expert')), may hold values from 0.2 to 1
- cotangent: bfloat16 [32768, 2048], P(('dp', 'expert')), may hold values from -1.5 to 1.5
- w_gate: bfloat16 [32, 2048, 768], P('expert'), may hold values from -0.125 to 0.125
- w_up: bfloat16 [32, 2048, 768], P('expert'), may hold values from -0.125 to 0.125
- w_down: bfloat16 [32, 768, 2048], P('expert'), may hold values from -0.21875 to 0.21875
Outputs:
- output: bfloat16 [32768, 2048], P(('dp', 'expert'))
- d_tokens: bfloat16 [32768, 2048], P(('dp', 'expert'))
- d_combine: float32 [32768, 4], P(('dp', 'expert'))
- d_w_gate: bfloat16 [32, 2048, 768], P('expert', 'dp')
- d_w_up: bfloat16 [32, 2048, 768], P('expert', 'dp')
- d_w_down: bfloat16 [32, 768, 2048], P('expert', None, 'dp')
The draws below stay inside these ranges and needn't reach their ends.
Inputs may be any that keep to these rules, and one draw needn't show every extreme that they name: `routes`: each row names 4 different experts. In the rows of one device (aligned blocks of 128 rows) no expert is named by more than 24 rows, a bound that some block reaches.
All inputs are finite; a program needn't handle non-finite values.
Results may differ from the reference program's by a relative error of at most 0.014.
Values may be sent and summed in bfloat16 or wider, within the bound.
A program may use at most 128 MiB of HBM per device.

```python
import math
import jax
import jax.numpy as jnp
import numpy as np
from jax import lax

D = 2048
FF = 768
TOP = 4
TOK_DEV = 128
EXPERTS = 32
CAP = 24
TOKENS = 32768
N_DP = 8
N_EXPERT = 32


def level_of(own_key, extent, shards, least, top_value):
    def one(dim, blocks):
        draws = jax.random.uniform(jax.random.fold_in(jax.random.fold_in(own_key, 6), dim), (blocks,), jnp.float32, least / len(shards), top_value / len(shards))
        return jnp.repeat(jnp.exp(draws), extent[dim] // blocks).reshape((-1,) + (1,) * (len(extent) - dim - 1))

    loudness = one(*shards[0])
    for cut in shards[1:]:
        loudness = loudness * one(*cut)
    return loudness


def routed_block(key, own, number, rows, count, top, bound, slope):
    order = jax.random.permutation(key, count)
    heavy_load, ordinary = portions_of(count, rows * top, bound, slope, True), portions_of(count, rows * top, bound, slope, False)
    places = jnp.arange(count)

    def named(lengths, rotation):
        used = int((lengths > 0).sum())
        fixed = max(1, used // 4)
        moved = fixed + (places - fixed + rotation * (used - fixed)) % max(1, count - fixed)
        return jnp.zeros((count,), jnp.int32).at[order[jnp.where(places < fixed, places, moved)]].set(jnp.asarray(lengths, jnp.int32))

    lengths = jnp.where(number % 4 == 0, named(heavy_load, number // 4), named(ordinary, number - number // 4 - 1))
    mixed = jax.random.permutation(jax.random.fold_in(own, 3), count)
    donor, receiver = mixed[0:count // 2 * 2:2], mixed[1:count // 2 * 2:2]
    margin = jnp.minimum(lengths[donor] - 1, bound - lengths[receiver]) // 2
    margin = jnp.where((donor == order[0]) | (receiver == order[0]) | (lengths[receiver] == 0), 0, jnp.maximum(margin, 0))
    moved = jax.random.randint(jax.random.fold_in(own, 4), (count // 2,), 0, 1 << 20) % (margin + 1)
    lengths = lengths.at[donor].add(-moved).at[receiver].add(moved)
    members = jnp.searchsorted(jnp.cumsum(lengths), jnp.arange(rows * top), side="right").astype(jnp.int32)
    table = members.reshape(top, rows).T
    table = table[jax.random.permutation(jax.random.fold_in(own, 1), rows)]
    rotation = jax.random.randint(jax.random.fold_in(own, 2), (rows, 1), 0, top)
    return jnp.take_along_axis(table, (jnp.arange(top)[None, :] + rotation) % top, axis=1)


def portions_of(number_of, total, bound, slope, full):
    weights = [(1 << 20) // math.isqrt(standing ** slope) + 1 for standing in range(1, number_of + 1)]
    largest = bound if full else min(bound, max(-(-total // number_of), total * weights[0] // sum(weights)))
    least = 1 if total - largest >= number_of - 1 else 0
    given, surplus = [largest] + [least] * (number_of - 1), total - largest - least * (number_of - 1)
    while surplus > 0:
        candidates = [i for i in range(1, number_of) if given[i] < largest] or [i for i in range(1, number_of) if given[i] < bound]
        pool, left = sum([weights[i] for i in candidates]), surplus
        for i in candidates:
            extra = min(bound - given[i], max(1, left * weights[i] // pool), surplus)
            given[i] = given[i] + extra
            surplus = surplus - extra
    return np.array(given)


def normal_values(rng, extent, deviation, most, shards=(), held_as=jnp.bfloat16):
    drawn = jax.random.normal(rng, extent, jnp.float32) * deviation
    if len(shards) > 0:
        drawn = level_of(rng, extent, shards, -0.22, 0.18) * drawn
    return jnp.clip(drawn, min=-most, max=most).astype(held_as)


def setup_inputs(seed: int = 0) -> dict:
    arg_keys = jax.random.split(jax.random.key(seed), 8)
    tokens = normal_values(arg_keys[0], (TOKENS, D), 1.0, 6.0, ((0, 256),))
    routes_keys = jax.random.split(jax.random.fold_in(arg_keys[1], 1), TOKENS // TOK_DEV)
    routes_turns = jax.random.permutation(jax.random.fold_in(arg_keys[1], 3), TOKENS // TOK_DEV)
    routes = jax.vmap(lambda own, number: routed_block(jax.random.fold_in(arg_keys[1], 2), own, number, TOK_DEV, EXPERTS, TOP, CAP, 2))(routes_keys, routes_turns).reshape((TOKENS, TOP))
    combine = jnp.clip(0.2 + 0.8 * jax.random.uniform(arg_keys[2], (TOKENS, TOP), jnp.float32) ** level_of(arg_keys[2], (TOKENS, TOP), ((0, 256),), -0.2, 0.2), 0.2, 1.0)
    cotangent = normal_values(arg_keys[3], (TOKENS, D), 0.25, 1.5, ((0, 256),))
    w_gate = normal_values(arg_keys[4], (EXPERTS, D, FF), D ** -0.5, 0.125, ((0, 32),))
    w_up = normal_values(arg_keys[5], (EXPERTS, D, FF), D ** -0.5, 0.125, ((0, 32),))
    w_down = normal_values(arg_keys[6], (EXPERTS, FF, D), FF ** -0.5, 0.21875, ((0, 32),))
    return {"tokens": tokens, "routes": routes, "combine": combine, "cotangent": cotangent, "w_gate": w_gate, "w_up": w_up, "w_down": w_down}


def slot_table(routes_dev, experts):
    flat_ids = routes_dev.reshape(-1)
    onehot = (flat_ids[:, None] == jnp.arange(experts, dtype=jnp.int32)[None, :]).astype(jnp.int32)
    before = jnp.cumsum(onehot, axis=0) - onehot
    return jnp.sum(before * onehot, axis=1).astype(jnp.int32)


def expert_step(pieces):
    rows_in, d_in, gate_w, up_w, down_w = pieces
    gate_pre = jnp.dot(rows_in, gate_w, preferred_element_type=jnp.float32)
    up_pre = jnp.dot(rows_in, up_w, preferred_element_type=jnp.float32)
    activated = jax.nn.silu(gate_pre)
    hidden = (activated * up_pre).astype(jnp.bfloat16)
    produced = jnp.dot(hidden, down_w, preferred_element_type=jnp.float32).astype(jnp.bfloat16)
    d_hidden = jnp.dot(d_in, down_w.T, preferred_element_type=jnp.float32)
    sigmoid_g = jax.nn.sigmoid(gate_pre)
    d_gate = (d_hidden * up_pre * sigmoid_g * (1.0 + gate_pre * (1.0 - sigmoid_g))).astype(jnp.bfloat16)
    d_up = (d_hidden * activated).astype(jnp.bfloat16)
    part_gate = jnp.dot(rows_in.T, d_gate, preferred_element_type=jnp.float32).astype(jnp.bfloat16)
    part_up = jnp.dot(rows_in.T, d_up, preferred_element_type=jnp.float32).astype(jnp.bfloat16)
    part_down = jnp.dot(hidden.T, d_in, preferred_element_type=jnp.float32).astype(jnp.bfloat16)
    d_rows = (jnp.dot(d_gate, gate_w.T, preferred_element_type=jnp.float32)
              + jnp.dot(d_up, up_w.T, preferred_element_type=jnp.float32)).astype(jnp.bfloat16)
    return produced, d_rows, part_gate, part_up, part_down


def reference(tokens, routes, combine, cotangent, w_gate, w_up, w_down):
    group_rows = TOK_DEV * N_EXPERT
    outputs = []
    d_tokens_all = []
    d_combine_all = []
    sum_gate = jnp.zeros((EXPERTS, D, FF), jnp.float32)
    sum_up = jnp.zeros((EXPERTS, D, FF), jnp.float32)
    sum_down = jnp.zeros((EXPERTS, FF, D), jnp.float32)
    for group in range(N_DP):
        tokens_g = tokens[group * group_rows:(group + 1) * group_rows]
        routes_g = routes[group * group_rows:(group + 1) * group_rows].reshape(N_EXPERT, TOK_DEV, TOP)
        combine_g = combine[group * group_rows:(group + 1) * group_rows]
        cot_g = cotangent[group * group_rows:(group + 1) * group_rows]
        slots = jax.vmap(slot_table, (0, None))(routes_g, EXPERTS)
        flat_ids = routes_g.reshape(N_EXPERT, TOK_DEV * TOP)
        source_dev = jnp.arange(N_EXPERT, dtype=jnp.int32)[:, None]
        target = (flat_ids * (N_EXPERT * CAP) + source_dev * CAP + slots).reshape(-1).astype(jnp.int32)
        pair_row = (source_dev * TOK_DEV + jnp.arange(TOK_DEV * TOP, dtype=jnp.int32)[None, :] // TOP).reshape(-1).astype(jnp.int32)
        rows_in = jnp.zeros((EXPERTS * N_EXPERT * CAP, D), jnp.bfloat16).at[target].set(tokens_g[pair_row])
        rows_in = rows_in.reshape(EXPERTS, N_EXPERT * CAP, D)
        scaled = (combine_g.reshape(-1)[:, None] * cot_g[pair_row].astype(jnp.float32)).astype(jnp.bfloat16)
        d_in = jnp.zeros((EXPERTS * N_EXPERT * CAP, D), jnp.bfloat16).at[target].set(scaled)
        d_in = d_in.reshape(EXPERTS, N_EXPERT * CAP, D)
        produced, d_rows, part_gate, part_up, part_down = lax.map(expert_step, (rows_in, d_in, w_gate, w_up, w_down))
        out_pair = produced.reshape(-1, D)[target].reshape(group_rows, TOP, D).astype(jnp.float32)
        outputs.append(jnp.sum(combine_g[:, :, None] * out_pair, axis=1).astype(jnp.bfloat16))
        d_combine_all.append(jnp.sum(out_pair * cot_g.astype(jnp.float32)[:, None, :], axis=2))
        back_pair = d_rows.reshape(-1, D)[target].reshape(group_rows, TOP, D).astype(jnp.float32)
        d_tokens_all.append(jnp.sum(back_pair, axis=1).astype(jnp.bfloat16))
        sum_gate = sum_gate + part_gate.astype(jnp.float32)
        sum_up = sum_up + part_up.astype(jnp.float32)
        sum_down = sum_down + part_down.astype(jnp.float32)
    return (jnp.concatenate(outputs, axis=0), jnp.concatenate(d_tokens_all, axis=0),
            jnp.concatenate(d_combine_all, axis=0), sum_gate.astype(jnp.bfloat16),
            sum_up.astype(jnp.bfloat16), sum_down.astype(jnp.bfloat16))
```

```python
import functools

import jax
import jax.numpy as jnp
from jax import lax
from jax.experimental import pallas as pl
from jax.experimental.pallas import tpu as pltpu
from jax.sharding import PartitionSpec as P

MESH = pl.DeviceIdType.MESH
NZ = 8
NX = 4
SUBS = 2
ORDER = [(0, 0), (1, 3), (0, 1), (1, 2), (0, 2), (1, 1), (0, 3), (1, 0)]
BF = jnp.bfloat16
F32 = jnp.float32


def place(m, tokens):
    return m // 2, pl.ds(tokens * (m % 2), tokens)


def neighbours():
    e = lax.axis_index("expert")
    x, z = e // NZ, e % NZ
    zp = x * NZ + (z + 1) % NZ
    zm = x * NZ + (z + NZ - 1) % NZ
    xp = ((x + 1) % NX) * NZ + z
    xm = ((x + NX - 1) % NX) * NZ + z
    return x, z, zp, zm, xp, xm


def greet(devices):
    barrier = pltpu.get_barrier_semaphore()
    for d in devices:
        pl.semaphore_signal(
            barrier, inc=1, device_id={"expert": d}, device_id_type=MESH
        )
    pl.semaphore_wait(barrier, len(devices))


def rcopy(src, dst, send, recv, dev):
    return pltpu.make_async_remote_copy(
        src_ref=src,
        dst_ref=dst,
        send_sem=send,
        recv_sem=recv,
        device_id={"expert": dev},
        device_id_type=MESH,
    )


def row_masks(meta, x, z, cap, blk):
    width = meta.shape[1]
    per = 2 * cap
    col = lax.broadcasted_iota(jnp.int32, (per, width), 1)
    row = lax.broadcasted_iota(jnp.int32, (per, width), 0)
    second = (row >= cap).astype(jnp.int32)
    shift = (col[0:1] >= width // 2).astype(jnp.int32) * 4096
    expert = ((x + blk + 1) % NX) * NZ + z
    ids = row - cap * second + 4096 * second + expert * cap
    return [ids == (meta[k : k + 1, :].astype(jnp.int32) + shift) for k in range(4)]


def dispatch_kernel(
    cap,
    tok_ref,
    cot_ref,
    rc_ref,
    rows_out,
    grad_out,
    picked_out,
    meta_out,
    ag,
    metab,
    smat,
    cmat,
    sx,
    r,
    relay,
    zs,
    zr,
    ms,
    mr,
    xs,
    xr,
    rs,
    rr,
    ls,
):
    tokens, features = tok_ref.shape
    hd = features // 2
    per = 2 * cap
    sub = tokens // SUBS
    x, z, zp, zm, xp, xm = neighbours()
    greet((zp, zm, xp, xm))
    srcs = (tok_ref, cot_ref)
    zdev = (zp, zm)

    def hop(h, s):
        return (s, s + 1) if h == 0 else ((NZ - s) % NZ, NZ - 1 - s)

    def zcopy(st, h, s, u):
        a, b = hop(h, s)
        if s == 0:
            src = srcs[st].at[pl.ds(sub * u, sub), pl.ds(h * hd, hd)]
        else:
            src = ag.at[st, h, a // 2, pl.ds(tokens * (a % 2) + sub * u, sub), :]
        dst = ag.at[st, h, b // 2, pl.ds(tokens * (b % 2) + sub * u, sub), :]
        return rcopy(src, dst, zs.at[st, h, s, u], zr.at[st, h, s, u], zdev[h])

    def mcopy(h, s):
        a, b = hop(h, s)
        (pa, la), (pb, lb) = place(a, tokens), place(b, tokens)
        return rcopy(
            metab.at[pa, :, la], metab.at[pb, :, lb], ms.at[h, s], mr.at[h, s], zdev[h]
        )

    meta_steps = (4, 3)

    def xcopy(st, h, p, i):
        half = pl.ds(h * hd, hd)
        block = (1, 0, 2)[i]
        if i == 0:
            dst = relay.at[st, h, p]
        else:
            dst = r.at[st, p * 4 + i - 1, :, half]
        return rcopy(
            sx.at[st, h, p, pl.ds(block * per, per), :],
            dst,
            xs.at[st, h, p, i],
            xr.at[st, h, p, i],
            (xp if h == 0 else xm, xp, xm)[i],
        )

    def fcopy(st, h, p):
        half = pl.ds(h * hd, hd)
        far = xp if h == 0 else xm
        return rcopy(
            relay.at[st, h, p], r.at[st, p * 4 + 2, :, half], rs.at[st, h, p], rr.at[st, h, p], far
        )

    for h in range(2):
        for u in range(SUBS):
            zcopy(0, h, 0, u).start()

    rc = rc_ref[...]
    experts = NX * NZ
    names = [rc[k : k + 1, :].astype(jnp.int32) for k in range(4)]
    ids = lax.broadcasted_iota(jnp.int32, (experts, tokens), 0)
    hits = [ids == n for n in names]
    count = sum(hit.astype(F32) for hit in hits)
    earlier = lax.broadcasted_iota(jnp.int32, (tokens, tokens), 0)
    later = lax.broadcasted_iota(jnp.int32, (tokens, tokens), 1)
    before = jnp.dot(
        count.astype(BF), (earlier < later).astype(F32).astype(BF), preferred_element_type=F32
    )
    for k in range(4):
        slot = jnp.sum(jnp.where(hits[k], before, 0.0), axis=0, keepdims=True)
        metab[0, k : k + 1, pl.ds(0, tokens)] = rc[k : k + 1, :] * cap + slot
    metab[0, 4:8, pl.ds(0, tokens)] = rc[4:8, :]
    for h in range(2):
        mcopy(h, 0).start()

    for st in range(2):
        for h in range(2):
            ag[st, h, 0, 0:tokens, :] = srcs[st][:, h * hd : (h + 1) * hd]

    ready = set()

    def masks(p):
        if p in ready:
            return
        ready.add(p)
        meta = metab[p]
        for blk in range(NX):
            hit = row_masks(meta, x, z, cap, blk)
            one = functools.reduce(jnp.logical_or, hit)
            weight = sum(jnp.where(hit[k], meta[4 + k : 5 + k, :], 0.0) for k in range(4))
            smat[p, blk * per : (blk + 1) * per, :] = one.astype(F32).astype(BF)
            cmat[p, blk * per : (blk + 1) * per, :] = jnp.broadcast_to(
                jnp.sum(weight, axis=1, keepdims=True), (per, 128)
            )

    def pick(st, h, p):
        masks(p)
        got = jnp.dot(smat[p], ag[st, h, p], preferred_element_type=F32)
        if st == 1:
            got = got * cmat[p, :, 0:1]
        got = got.astype(BF)
        sx[st, h, p] = got
        r[st, p * 4 + 3, :, h * hd : (h + 1) * hd] = got[3 * per :]
        for i in range(3):
            xcopy(st, h, p, i).start()

    def forward(st, h, p):
        xcopy(st, h, p, 0).wait_recv()
        fcopy(st, h, p).start()

    done = {1: [(0, 0)], 2: [(1, 3)], 3: [(0, 1)], 4: [(1, 2)], 5: [(0, 2)], 6: [(1, 1)], 7: [(0, 3), (1, 0)]}
    pending = []
    for st in range(2):
        for d in range(1, NZ):
            if st == 0:
                for h in range(2):
                    if d <= meta_steps[h]:
                        mcopy(h, d - 1).wait_recv()
                        if d < meta_steps[h]:
                            mcopy(h, d).start()
            for u in range(SUBS):
                for h in range(2):
                    zcopy(st, h, d - 1, u).wait_recv()
                    if d < NZ - 1:
                        zcopy(st, h, d, u).start()
                    elif st == 0:
                        zcopy(1, h, 0, u).start()
            for item in pending:
                forward(*item)
            pending = []
            for h, p in done[d]:
                pick(st, h, p)
                pending.append((st, h, p))
    for item in pending:
        forward(*item)

    outs = []
    for st in range(2):
        for h, p in ORDER:
            for i in (1, 2):
                xcopy(st, h, p, i).wait_recv()
            fcopy(st, h, p).wait_recv()
        out = (rows_out, grad_out)[st]
        c = pltpu.make_async_copy(r.at[st], out, ls.at[st])
        c.start()
        outs.append(c)
    for src, dst, i in ((sx.at[1], picked_out, 2), (metab, meta_out, 3)):
        c = pltpu.make_async_copy(src, dst, ls.at[i])
        c.start()
        outs.append(c)
    for st in range(2):
        for h in range(2):
            for s in range(NZ - 1):
                for u in range(SUBS):
                    zcopy(st, h, s, u).wait_send()
        for h, p in ORDER:
            for i in range(3):
                xcopy(st, h, p, i).wait_send()
            fcopy(st, h, p).wait_send()
    for h in range(2):
        for s in range(meta_steps[h]):
            mcopy(h, s).wait_send()
    for c in outs:
        c.wait()


def dispatch(tokens, cotangent, rc, cap):
    n, features = tokens.shape
    hd = features // 2
    per = 2 * cap
    dma = pltpu.SemaphoreType.DMA
    vmem = pl.BlockSpec(memory_space=pltpu.VMEM)
    hbm = pl.BlockSpec(memory_space=pl.ANY)
    return pl.pallas_call(
        functools.partial(dispatch_kernel, cap),
        out_shape=(
            jax.ShapeDtypeStruct((16, per, features), BF),
            jax.ShapeDtypeStruct((16, per, features), BF),
            jax.ShapeDtypeStruct((2, 4, 4 * per, hd), BF),
            jax.ShapeDtypeStruct((4, 8, 2 * n), F32),
        ),
        in_specs=[vmem] * 3,
        out_specs=(hbm,) * 4,
        scratch_shapes=[
            pltpu.VMEM((2, 2, 4, 2 * n, hd), BF),
            pltpu.VMEM((4, 8, 2 * n), F32),
            pltpu.VMEM((4, 4 * per, 2 * n), BF),
            pltpu.VMEM((4, 4 * per, 128), F32),
            pltpu.VMEM((2, 2, 4, 4 * per, hd), BF),
            pltpu.VMEM((2, 16, per, features), BF),
            pltpu.VMEM((2, 2, 4, per, hd), BF),
            dma((2, 2, NZ - 1, SUBS)),
            dma((2, 2, NZ - 1, SUBS)),
            dma((2, 4)),
            dma((2, 4)),
            dma((2, 2, 4, 3)),
            dma((2, 2, 4, 3)),
            dma((2, 2, 4)),
            dma((2, 2, 4)),
            dma((4,)),
        ],
        compiler_params=pltpu.CompilerParams(
            collective_id=0, has_side_effects=True, vmem_limit_bytes=60 * 1024 * 1024
        ),
        name="dispatch",
    )(tokens, cotangent, rc)


def return_kernel(
    cap,
    prod_ref,
    drow_ref,
    picked_ref,
    meta_ref,
    out_ref,
    dtok_ref,
    dcomb_ref,
    q,
    relay,
    part,
    land,
    smat,
    scmat,
    dacc,
    dland,
    zs,
    zr,
    ds_,
    dr,
    xs,
    xr,
    rs,
    rr,
):
    tokens = out_ref.shape[0]
    features = out_ref.shape[1]
    hd = features // 2
    per = 2 * cap
    sub = tokens // SUBS
    x, z, zp, zm, xp, xm = neighbours()
    greet((zp, zm, xp, xm))
    srcs = (prod_ref, drow_ref)
    zdev = (zp, zm)

    def xcopy(st, h, p, i):
        half = pl.ds(h * hd, hd)
        if i == 0:
            dst = relay.at[st, h, p]
        else:
            dst = q.at[st, p, pl.ds((0, 2)[i - 1] * per, per), half]
        return rcopy(
            srcs[st].at[p * 4 + (2, 0, 1)[i], :, half],
            dst,
            xs.at[st, h, p, i],
            xr.at[st, h, p, i],
            (xp if h == 0 else xm, xm, xp)[i],
        )

    def fcopy(st, h, p):
        half = pl.ds(h * hd, hd)
        far = xp if h == 0 else xm
        return rcopy(
            relay.at[st, h, p],
            q.at[st, p, pl.ds(per, per), half],
            rs.at[st, h, p],
            rr.at[st, h, p],
            far,
        )

    def chunk(h, s):
        return s + 1 if h == 0 else NZ - 1 - s

    def zcopy(st, h, s, u):
        m = chunk(h, s)
        src = part.at[st, h, m // 2, pl.ds(tokens * (m % 2) + sub * u, sub), :]
        dst = land.at[st, h, s, pl.ds(sub * u, sub), :]
        return rcopy(src, dst, zs.at[st, h, s, u], zr.at[st, h, s, u], zdev[h])

    def dcopy(s):
        m = s + 1
        pm, lm = place(m, tokens)
        return rcopy(dacc.at[pm, :, lm], dland.at[s], ds_.at[s], dr.at[s], zp)

    for st in range(2):
        for h, p in ORDER:
            for i in range(3):
                xcopy(st, h, p, i).start()

    for p in range(4):
        meta = meta_ref[p]
        for blk in range(NX):
            hit = row_masks(meta, x, z, cap, blk)
            one = functools.reduce(jnp.logical_or, hit)
            weight = sum(jnp.where(hit[k], meta[4 + k : 5 + k, :], 0.0) for k in range(4))
            smat[p, blk * per : (blk + 1) * per, :] = one.astype(F32).astype(BF)
            scmat[p, blk * per : (blk + 1) * per, :] = weight.astype(BF)
        for st in range(2):
            q[st, p, 3 * per :, :] = srcs[st][p * 4 + 3]

    def forward(st, h, p):
        xcopy(st, h, p, 0).wait_recv()
        fcopy(st, h, p).start()

    def scatter(st, h, p):
        for i in (1, 2):
            xcopy(st, h, p, i).wait_recv()
        fcopy(st, h, p).wait_recv()
        mat = scmat if st == 0 else smat
        part[st, h, p] = lax.dot_general(
            mat[p],
            q[st, p, :, h * hd : (h + 1) * hd],
            (((0,), (0,)), ((), ())),
            preferred_element_type=F32,
        ).astype(BF)

    def ring(st, h, s):
        m = chunk(h, s + 1) % NZ
        for u in range(SUBS):
            zcopy(st, h, s, u).wait_recv()
            rows = pl.ds(tokens * (m % 2) + sub * u, sub)
            total = (
                land[st, h, s, pl.ds(sub * u, sub), :].astype(F32)
                + part[st, h, m // 2, rows, :].astype(F32)
            ).astype(BF)
            if s < NZ - 2:
                part[st, h, m // 2, rows, :] = total
                zcopy(st, h, s + 1, u).start()
            else:
                out = (out_ref, dtok_ref)[st]
                out[pl.ds(sub * u, sub), pl.ds(h * hd, hd)] = total

    def weights():
        for p in range(4):
            meta = meta_ref[p]
            for k in range(4):
                dacc[p, k : k + 1, :] = jnp.zeros((1, 2 * tokens), F32)
            dacc[p, 4:8, :] = jnp.zeros((4, 2 * tokens), F32)
            for blk in range(NX):
                rows = pl.ds(blk * per, per)
                v = jnp.zeros((per, 1), F32)
                for h in range(2):
                    a = q[0, p, rows, h * hd : (h + 1) * hd].astype(F32)
                    b = picked_ref[h, p, rows, :].astype(F32)
                    v = v + jnp.sum(a * b, axis=1, keepdims=True)
                hit = row_masks(meta, x, z, cap, blk)
                w = sum(jnp.where(hit[k], meta[4 + k : 5 + k, :], 0.0) for k in range(4))
                c = jnp.sum(w, axis=1, keepdims=True)
                v = v / jnp.where(c > 0.0, c, 1.0)
                for k in range(4):
                    dacc[p, k : k + 1, :] += jnp.sum(
                        jnp.where(hit[k], v, 0.0), axis=0, keepdims=True
                    )

    forward(0, *ORDER[0])
    for st in range(2):
        for i, (h, p) in enumerate(ORDER):
            if i + 1 < len(ORDER):
                forward(st, *ORDER[i + 1])
            elif st == 0:
                forward(1, *ORDER[0])
            scatter(st, h, p)
            if i < 2:
                for u in range(SUBS):
                    zcopy(st, h, 0, u).start()
                if st == 1 and i == 1:
                    for hh in range(2):
                        ring(0, hh, NZ - 2)
                    weights()
                    dcopy(0).start()
            else:
                for hh in range(2):
                    ring(st, hh, i - 2)
                if st == 1:
                    s = i - 2
                    dcopy(s).wait_recv()
                    pm, lm = place(s + 2 if s < NZ - 2 else 0, tokens)
                    dacc[pm, :, lm] += dland[s]
                    dcopy(s + 1).start()
    for hh in range(2):
        ring(1, hh, NZ - 2)
    dcopy(NZ - 2).wait_recv()
    dcomb_ref[...] = dacc[0, :, pl.ds(0, tokens)] + dland[NZ - 2]

    for st in range(2):
        for h in range(2):
            for s in range(NZ - 1):
                for u in range(SUBS):
                    zcopy(st, h, s, u).wait_send()
        for h, p in ORDER:
            for i in range(3):
                xcopy(st, h, p, i).wait_send()
            fcopy(st, h, p).wait_send()
    for s in range(NZ - 1):
        dcopy(s).wait_send()


def give_back(produced, d_rows, picked, meta, tokens, cap):
    features = produced.shape[2]
    hd = features // 2
    per = 2 * cap
    dma = pltpu.SemaphoreType.DMA
    vmem = pl.BlockSpec(memory_space=pltpu.VMEM)
    return pl.pallas_call(
        functools.partial(return_kernel, cap),
        out_shape=(
            jax.ShapeDtypeStruct((tokens, features), BF),
            jax.ShapeDtypeStruct((tokens, features), BF),
            jax.ShapeDtypeStruct((8, tokens), F32),
        ),
        in_specs=[vmem] * 4,
        out_specs=(vmem,) * 3,
        scratch_shapes=[
            pltpu.VMEM((2, 4, 4 * per, features), BF),
            pltpu.VMEM((2, 2, 4, per, hd), BF),
            pltpu.VMEM((2, 2, 4, 2 * tokens, hd), BF),
            pltpu.VMEM((2, 2, NZ - 1, tokens, hd), BF),
            pltpu.VMEM((4, 4 * per, 2 * tokens), BF),
            pltpu.VMEM((4, 4 * per, 2 * tokens), BF),
            pltpu.VMEM((4, 8, 2 * tokens), F32),
            pltpu.VMEM((NZ - 1, 8, tokens), F32),
            dma((2, 2, NZ - 1, SUBS)),
            dma((2, 2, NZ - 1, SUBS)),
            dma((NZ - 1,)),
            dma((NZ - 1,)),
            dma((2, 2, 4, 3)),
            dma((2, 2, 4, 3)),
            dma((2, 2, 4)),
            dma((2, 2, 4)),
        ],
        compiler_params=pltpu.CompilerParams(
            collective_id=1, has_side_effects=True, vmem_limit_bytes=60 * 1024 * 1024
        ),
        name="give_back",
    )(produced, d_rows, picked, meta)


def per_device(tokens, routes, combine, cotangent, w_gate, w_up, w_down):
    n, features = tokens.shape
    per_token = routes.shape[1]
    experts = w_gate.shape[0] * lax.axis_size("expert")
    cap = 3 * n * per_token // (2 * experts)
    rc = jnp.concatenate([routes.T.astype(F32), combine.T], axis=0)
    rows3, grad3, picked, meta = dispatch(tokens, cotangent, rc, cap)
    rows, d_in = rows3.reshape(-1, features), grad3.reshape(-1, features)
    w_gate, w_up, w_down = w_gate[0], w_up[0], w_down[0]
    gate_pre = jnp.dot(rows, w_gate, preferred_element_type=F32)
    up_pre = jnp.dot(rows, w_up, preferred_element_type=F32)
    activated = jax.nn.silu(gate_pre)
    hidden = (activated * up_pre).astype(BF)
    produced = jnp.dot(hidden, w_down, preferred_element_type=F32).astype(BF)
    d_hidden = jnp.dot(d_in, w_down.T, preferred_element_type=F32)
    sig = jax.nn.sigmoid(gate_pre)
    d_gate = (d_hidden * up_pre * sig * (1.0 + gate_pre * (1.0 - sig))).astype(BF)
    d_up = (d_hidden * activated).astype(BF)
    d_rows = (
        jnp.dot(d_gate, w_gate.T, preferred_element_type=F32)
        + jnp.dot(d_up, w_up.T, preferred_element_type=F32)
    ).astype(BF)
    part_down = jnp.dot(hidden.T, d_in, preferred_element_type=F32).astype(BF)
    part_gate = jnp.dot(rows.T, d_gate, preferred_element_type=F32).astype(BF)
    part_up = jnp.dot(rows.T, d_up, preferred_element_type=F32).astype(BF)
    d_w_gate = lax.psum_scatter(part_gate[None], "dp", scatter_dimension=1, tiled=True)
    d_w_up = lax.psum_scatter(part_up[None], "dp", scatter_dimension=1, tiled=True)
    d_w_down = lax.psum_scatter(part_down[None], "dp", scatter_dimension=2, tiled=True)
    output, d_tokens, d_comb = give_back(
        produced.reshape(rows3.shape), d_rows.reshape(rows3.shape), picked, meta, n, cap
    )
    return output, d_tokens, d_comb[:per_token].T, d_w_gate, d_w_up, d_w_down


def solution(mesh):
    row = P(("dp", "expert"), None)
    weight = P("expert", None, None)
    return jax.shard_map(
        per_device,
        mesh=mesh,
        in_specs=(row, row, row, row, weight, weight, weight),
        out_specs=(
            row,
            row,
            row,
            P("expert", "dp", None),
            P("expert", "dp", None),
            P("expert", None, "dp"),
        ),
        check_vma=False,
    )
```

```python
import functools

import jax
import jax.numpy as jnp
from jax import lax
from jax.experimental import pallas as pl
from jax.experimental.pallas import tpu as pltpu
from jax.sharding import PartitionSpec as P

MESH = pl.DeviceIdType.MESH
NZ = 8
NX = 4
SUBS = 4
BF = jnp.bfloat16
F32 = jnp.float32


def neighbours():
    e = lax.axis_index("expert")
    x, z = e // NZ, e % NZ
    zp = x * NZ + (z + 1) % NZ
    zm = x * NZ + (z + NZ - 1) % NZ
    xp = ((x + 1) % NX) * NZ + z
    xm = ((x + NX - 1) % NX) * NZ + z
    return x, z, zp, zm, xp, xm


def greet(devices):
    barrier = pltpu.get_barrier_semaphore()
    for d in devices:
        pl.semaphore_signal(
            barrier, inc=1, device_id={"expert": d}, device_id_type=MESH
        )
    pl.semaphore_wait(barrier, len(devices))


def rcopy(src, dst, send, recv, dev):
    return pltpu.make_async_remote_copy(
        src_ref=src,
        dst_ref=dst,
        send_sem=send,
        recv_sem=recv,
        device_id={"expert": dev},
        device_id_type=MESH,
    )


def row_masks(meta, x, z, cap, blk):
    width = meta.shape[1]
    per = 2 * cap
    col = lax.broadcasted_iota(jnp.int32, (per, width), 1)
    row = lax.broadcasted_iota(jnp.int32, (per, width), 0)
    second = (row >= cap).astype(jnp.int32)
    shift = (col[0:1] >= width // 2).astype(jnp.int32) * 4096
    expert = ((x + blk + 1) % NX) * NZ + z
    ids = row - cap * second + 4096 * second + expert * cap
    return [ids == (meta[k : k + 1, :].astype(jnp.int32) + shift) for k in range(4)]


def dispatch_kernel(
    cap,
    tok_ref,
    cot_ref,
    rc_ref,
    wg_ref,
    wu_ref,
    wd_ref,
    rows_out,
    grad_out,
    picked_out,
    meta_out,
    hid_out,
    dga_out,
    act_out,
    prod_out,
    ag,
    metab,
    smat,
    cmat,
    sx,
    r,
    relay,
    wg,
    wu,
    wd,
    gate,
    hid,
    dga,
    act,
    prod,
    zs,
    zr,
    ms,
    mr,
    xs,
    xr,
    rs,
    rr,
    ls,
    ws,
    os_,
):
    tokens, features = tok_ref.shape
    ff = wg_ref.shape[1]
    hd = features // 2
    per = 2 * cap
    sub = tokens // SUBS
    ft = ff // 3
    nt = features // 4
    x, z, zp, zm, xp, xm = neighbours()
    zdev = (zp, zm)

    loads = []
    for st, src in enumerate((tok_ref, cot_ref)):
        for h in range(2):
            c = pltpu.make_async_copy(
                src.at[:, pl.ds(h * hd, hd)],
                ag.at[st, h, pl.ds(0, tokens), :],
                ls.at[st, h],
            )
            c.start()
            loads.append(c)

    def wload(i, f):
        if i == 2:
            return pltpu.make_async_copy(wd_ref.at[:, pl.ds(f * nt, nt)], wd.at[f], ws.at[i, f])
        src, dst = ((wg_ref, wg), (wu_ref, wu))[i]
        return pltpu.make_async_copy(src.at[:, pl.ds(f * ft, ft)], dst.at[f], ws.at[i, f])

    greet((zp, zm, xp, xm))

    def zcopy(st, h, s, u):
        a = s if h == 0 else (NZ - s) % NZ
        b = s + 1 if h == 0 else NZ - 1 - s
        src = ag.at[st, h, pl.ds(pl.multiple_of(a * tokens + sub * u, sub), sub), :]
        dst = ag.at[st, h, pl.ds(pl.multiple_of(b * tokens + sub * u, sub), sub), :]
        return rcopy(src, dst, zs.at[st, h, s, u], zr.at[st, h, s, u], zdev[h])

    def mcopy(h, s):
        a = s if h == 0 else (NZ - s) % NZ
        b = s + 1 if h == 0 else NZ - 1 - s
        return rcopy(metab.at[a], metab.at[b], ms.at[h, s], mr.at[h, s], zdev[h])

    def xcopy(st, h, p, i):
        far = jnp.where(h == 0, xp, xm)
        dst = relay.at[st, h, p] if i == 0 else r.at[st, h, p * 4 + i - 1]
        return rcopy(
            sx.at[st, h, p, pl.ds((1, 0, 2)[i] * per, per), :],
            dst,
            xs.at[st, h, p, i],
            xr.at[st, h, p, i],
            (far, xp, xm)[i],
        )

    def fcopy(st, h, p):
        far = jnp.where(h == 0, xp, xm)
        return rcopy(relay.at[st, h, p], r.at[st, h, p * 4 + 2], rs.at[st, h, p], rr.at[st, h, p], far)

    for h in range(2):
        loads[h].wait()
        for u in range(SUBS):
            zcopy(0, h, 0, u).start()
    for i, n in ((0, 3), (1, 3), (2, 4)):
        for f in range(n):
            wload(i, f).start()

    rc = rc_ref[...]
    experts = NX * NZ
    names = [rc[k : k + 1, :].astype(jnp.int32) for k in range(4)]
    ids = lax.broadcasted_iota(jnp.int32, (experts, tokens), 0)
    hits = [ids == n for n in names]
    count = sum(hit.astype(F32) for hit in hits)
    earlier = lax.broadcasted_iota(jnp.int32, (tokens, tokens), 0)
    later = lax.broadcasted_iota(jnp.int32, (tokens, tokens), 1)
    before = jnp.dot(
        count.astype(BF), (earlier < later).astype(F32).astype(BF), preferred_element_type=F32
    )
    for k in range(4):
        slot = jnp.sum(jnp.where(hits[k], before, 0.0), axis=0, keepdims=True)
        metab[0, k : k + 1, :] = rc[k : k + 1, :] * cap + slot
    metab[0, 4:8, :] = rc[4:8, :]
    for h in range(2):
        mcopy(h, 0).start()
    for c in loads[2:]:
        c.wait()

    def masks(p):
        meta = jnp.concatenate([metab[2 * p], metab[2 * p + 1]], axis=1)
        for blk in range(NX):
            hit = row_masks(meta, x, z, cap, blk)
            one = functools.reduce(jnp.logical_or, hit)
            weight = sum(jnp.where(hit[k], meta[4 + k : 5 + k, :], 0.0) for k in range(4))
            smat[p, blk * per : (blk + 1) * per, :] = one.astype(F32).astype(BF)
            cmat[p, blk * per : (blk + 1) * per, :] = jnp.broadcast_to(
                jnp.sum(weight, axis=1, keepdims=True), (per, 128)
            )

    def where_at(t):
        st, j = t // 8, t % 8
        h = j % 2
        return st, j, h, jnp.where(h == 0, j // 2, 3 - j // 2)

    def forward(t):
        st, _, h, p = where_at(t)
        xcopy(st, h, p, 0).wait_recv()
        fcopy(st, h, p).start()

    def arrived(st):
        @pl.loop(0, 8)
        def _(i):
            h, p = i // 4, i % 4
            for k in (1, 2):
                xcopy(st, h, p, k).wait_recv()
            fcopy(st, h, p).wait_recv()

    def project(w, f):
        a = jnp.dot(r[0, 0].reshape(-1, hd), w[f, 0:hd], preferred_element_type=F32)
        return a + jnp.dot(r[0, 1].reshape(-1, hd), w[f, hd:], preferred_element_type=F32)

    def gate_tile(f):
        gate[...] = project(wg, f)

    def up_tile(f):
        up = project(wu, f)
        g = gate[...]
        sig = 1.0 / (1.0 + jnp.exp(-g))
        a = g * sig
        act[f] = a.astype(BF)
        hid[f] = (a * up).astype(BF)
        dga[f] = (up * sig * (1.0 + g * (1.0 - sig))).astype(BF)

    def down_tile(h, part):
        n = 2 * h + part
        out = sum(
            jnp.dot(hid[f], wd[n, f * ft : (f + 1) * ft], preferred_element_type=F32)
            for f in range(3)
        )
        prod[h, :, :, part * nt : (part + 1) * nt] = out.astype(BF).reshape(16, per, nt)

    def ring(t, us):
        st, j, _, _ = where_at(t)

        @pl.when(j < NZ - 1)
        def _():
            for u in us:
                for h in range(2):
                    zcopy(st, h, j, u).wait_recv()

                    @pl.when(j < NZ - 2)
                    def _():
                        zcopy(st, h, j + 1, u).start()

                    @pl.when((j == NZ - 2) & (st == 0))
                    def _():
                        zcopy(1, h, 0, u).start()

    @pl.loop(0, 16)
    def _(t):
        st, j, h, p = where_at(t)

        @pl.when(st == 0)
        def _():
            for hh, n in ((0, 4), (1, 3)):

                @pl.when(j < n)
                def _():
                    mcopy(hh, j).wait_recv()

                @pl.when(j + 1 < n)
                def _():
                    mcopy(hh, j + 1).start()

        ring(t, range(0, SUBS // 2))

        @pl.when(t == 10)
        def _():
            arrived(0)
            for i, n in ((0, 3), (1, 3), (2, 4)):
                for f in range(n):
                    wload(i, f).wait()

        tile = (st == 1) & (j >= 2) & (j < 5)
        down = (st == 1) & (j >= 5) & (j < 7)

        @pl.when(tile)
        def _():
            gate_tile(j - 2)

        @pl.when(down)
        def _():
            down_tile(j - 5, 0)

        ring(t, range(SUBS // 2, SUBS))

        @pl.when(t > 0)
        def _():
            forward(t - 1)

        @pl.when(t < 4)
        def _():
            masks(p)

        got = jnp.dot(
            smat[p],
            ag[st, h, pl.ds(pl.multiple_of(p * 2 * tokens, 2 * tokens), 2 * tokens), :],
            preferred_element_type=F32,
        )
        got = (got * jnp.where(st == 1, cmat[p, :, 0:1], 1.0)).astype(BF)
        sx[st, h, p] = got
        r[st, h, p * 4 + 3] = got[3 * per :]
        for i in range(3):
            xcopy(st, h, p, i).start()

        @pl.when(tile)
        def _():
            up_tile(j - 2)

        @pl.when(down)
        def _():
            down_tile(j - 5, 1)

    outs = [(hid, hid_out), (dga, dga_out), (act, act_out), (prod, prod_out), (r.at[0], rows_out), (metab, meta_out), (sx.at[1], picked_out)]
    for i, (src, dst) in enumerate(outs):
        pltpu.make_async_copy(src, dst, os_.at[i]).start()
    forward(15)
    arrived(1)
    last = pltpu.make_async_copy(r.at[1], grad_out, os_.at[len(outs)])
    last.start()

    @pl.loop(0, 2)
    def _(st):
        for h in range(2):

            @pl.loop(0, NZ - 1)
            def _(s):
                for u in range(SUBS):
                    zcopy(st, h, s, u).wait_send()

        @pl.loop(0, 8)
        def _(i):
            for k in range(3):
                xcopy(st, i // 4, i % 4, k).wait_send()
            fcopy(st, i // 4, i % 4).wait_send()

    for h, n in ((0, 4), (1, 3)):
        for s in range(n):
            mcopy(h, s).wait_send()
    for i, (src, dst) in enumerate(outs):
        pltpu.make_async_copy(src, dst, os_.at[i]).wait()
    last.wait()


def dispatch(tokens, cotangent, rc, w_gate, w_up, w_down, cap):
    n, features = tokens.shape
    ff = w_gate.shape[1]
    hd = features // 2
    per = 2 * cap
    rows = 16 * per
    ft, nt = ff // 3, features // 4
    dma = pltpu.SemaphoreType.DMA
    vmem = pl.BlockSpec(memory_space=pltpu.VMEM)
    hbm = pl.BlockSpec(memory_space=pl.ANY)
    halves = jax.ShapeDtypeStruct((2, 16, per, hd), BF)
    hidden = jax.ShapeDtypeStruct((3, rows, ft), BF)
    return pl.pallas_call(
        functools.partial(dispatch_kernel, cap),
        out_shape=(
            halves,
            halves,
            jax.ShapeDtypeStruct((2, 4, 4 * per, hd), BF),
            jax.ShapeDtypeStruct((NZ, 8, n), F32),
            hidden,
            hidden,
            hidden,
            halves,
        ),
        in_specs=[hbm, hbm, vmem, hbm, hbm, hbm],
        out_specs=(hbm,) * 8,
        scratch_shapes=[
            pltpu.VMEM((2, 2, NZ * n, hd), BF),
            pltpu.VMEM((NZ, 8, n), F32),
            pltpu.VMEM((4, 4 * per, 2 * n), BF),
            pltpu.VMEM((4, 4 * per, 128), F32),
            pltpu.VMEM((2, 2, 4, 4 * per, hd), BF),
            pltpu.VMEM((2, 2, 16, per, hd), BF),
            pltpu.VMEM((2, 2, 4, per, hd), BF),
            pltpu.VMEM((3, features, ft), BF),
            pltpu.VMEM((3, features, ft), BF),
            pltpu.VMEM((4, ff, nt), BF),
            pltpu.VMEM((rows, ft), F32),
            pltpu.VMEM((3, rows, ft), BF),
            pltpu.VMEM((3, rows, ft), BF),
            pltpu.VMEM((3, rows, ft), BF),
            pltpu.VMEM((2, 16, per, hd), BF),
            dma((2, 2, NZ - 1, SUBS)),
            dma((2, 2, NZ - 1, SUBS)),
            dma((2, 4)),
            dma((2, 4)),
            dma((2, 2, 4, 3)),
            dma((2, 2, 4, 3)),
            dma((2, 2, 4)),
            dma((2, 2, 4)),
            dma((2, 2)),
            dma((3, 4)),
            dma((8,)),
        ],
        compiler_params=pltpu.CompilerParams(
            collective_id=0, has_side_effects=True, vmem_limit_bytes=62 * 1024 * 1024
        ),
        name="dispatch",
    )(tokens, cotangent, rc, w_gate, w_up, w_down)


def return_kernel(
    cap,
    prod_ref,
    drow_ref,
    picked_ref,
    meta_ref,
    out_ref,
    dtok_ref,
    dcomb_ref,
    q,
    relay,
    part,
    land,
    smat,
    stmat,
    dacc,
    dland,
    zs,
    zr,
    ds_,
    dr,
    xs,
    xr,
    rs,
    rr,
    ls,
):
    tokens, features = out_ref.shape
    hd = features // 2
    per = 2 * cap
    sub = tokens // SUBS
    x, z, zp, zm, xp, xm = neighbours()
    zdev = (zp, zm)
    srcs = (prod_ref, drow_ref)
    greet((zp, zm, xp, xm))

    def where_at(t):
        st, j = t // 8, t % 8
        h = j % 2
        return st, j, h, jnp.where(h == 0, j // 2, 3 - j // 2)

    def xcopy(st, h, p, i, src):
        far = jnp.where(h == 0, xp, xm)
        dst = relay.at[st, h, p] if i == 0 else q.at[st, h, p, pl.ds((0, 2)[i - 1] * per, per), :]
        return rcopy(
            src.at[h, p * 4 + (2, 0, 1)[i]],
            dst,
            xs.at[st, h, p, i],
            xr.at[st, h, p, i],
            (far, xm, xp)[i],
        )

    def fcopy(st, h, p):
        far = jnp.where(h == 0, xp, xm)
        return rcopy(
            relay.at[st, h, p],
            q.at[st, h, p, pl.ds(per, per), :],
            rs.at[st, h, p],
            rr.at[st, h, p],
            far,
        )

    def own(st, h, p, src):
        return pltpu.make_async_copy(
            src.at[h, p * 4 + 3], q.at[st, h, p, pl.ds(3 * per, per), :], ls.at[st, h, p]
        )

    def send(t):
        st, _, h, p = where_at(t)
        for i in range(2):

            @pl.when(st == i)
            def _():
                for k in range(3):
                    xcopy(i, h, p, k, srcs[i]).start()
                own(i, h, p, srcs[i]).start()

    def forward(t):
        st, _, h, p = where_at(t)
        xcopy(st, h, p, 0, prod_ref).wait_recv()
        fcopy(st, h, p).start()

    def chunk(h, s):
        return s + 1 if h == 0 else NZ - 1 - s

    def zcopy(st, h, s, u):
        m = chunk(h, s)
        src = part.at[st, h, pl.ds(pl.multiple_of(m * tokens + sub * u, sub), sub), :]
        dst = land.at[st, h, s, pl.ds(sub * u, sub), :]
        return rcopy(src, dst, zs.at[st, h, s, u], zr.at[st, h, s, u], zdev[h])

    def dcopy(s):
        return rcopy(dacc.at[s + 1], dland.at[s], ds_.at[s], dr.at[s], zp)

    def meta_of(p):
        return jnp.concatenate([meta_ref[2 * p], meta_ref[2 * p + 1]], axis=1)

    def mats(p):
        meta = meta_of(p)
        for blk in range(NX):
            hit = row_masks(meta, x, z, cap, blk)
            one = functools.reduce(jnp.logical_or, hit)
            weight = sum(jnp.where(hit[k], meta[4 + k : 5 + k, :], 0.0) for k in range(4))
            smat[0, blk * per : (blk + 1) * per, :] = weight
            smat[1, blk * per : (blk + 1) * per, :] = one.astype(F32)
        for i in range(2):
            stmat[i, p] = smat[i].T.astype(BF)

    def scatter(t):
        st, _, h, p = where_at(t)
        for k in (1, 2):
            xcopy(st, h, p, k, prod_ref).wait_recv()
        fcopy(st, h, p).wait_recv()
        own(st, h, p, prod_ref).wait()
        rows = pl.ds(pl.multiple_of(p * 2 * tokens, 2 * tokens), 2 * tokens)
        part[st, h, rows, :] = jnp.dot(
            stmat[st, p], q[st, h, p], preferred_element_type=F32
        ).astype(BF)

    def ring(st, s, us):
        for u in us:
            for h in range(2):
                m = chunk(h, s + 1)
                rows = pl.ds(pl.multiple_of(m * tokens + sub * u, sub), sub)
                zcopy(st, h, s, u).wait_recv()
                part[st, h, rows, :] += land[st, h, s, pl.ds(sub * u, sub), :]
                zcopy(st, h, s + 1, u).start()

    def finish(st, us):
        out = (out_ref, dtok_ref)[st]
        for u in us:
            rows = pl.ds(sub * u, sub)
            for h in range(2):
                zcopy(st, h, NZ - 2, u).wait_recv()
                out[rows, h * hd : (h + 1) * hd] = part[st, h, rows, :] + land[st, h, NZ - 2, rows, :]

    def weights(p):
        meta = meta_of(p)
        total = [jnp.zeros((1, 2 * tokens), F32)] * 4
        for blk in range(NX):
            v = jnp.zeros((per, 1), F32)
            for h in range(2):
                a = q[0, h, p, blk * per : (blk + 1) * per, :].astype(F32)
                b = picked_ref[h, p, blk * per : (blk + 1) * per, :].astype(F32)
                v = v + jnp.sum(a * b, axis=1, keepdims=True)
            hit = row_masks(meta, x, z, cap, blk)
            w = sum(jnp.where(hit[k], meta[4 + k : 5 + k, :], 0.0) for k in range(4))
            c = jnp.sum(w, axis=1, keepdims=True)
            v = v / jnp.where(c > 0.0, c, 1.0)
            for k in range(4):
                total[k] = total[k] + jnp.sum(jnp.where(hit[k], v, 0.0), axis=0, keepdims=True)
        for k in range(4):
            for i in range(2):
                dacc[2 * p + i, k : k + 1, :] = total[k][:, i * tokens : (i + 1) * tokens]
        for i in range(2):
            dacc[2 * p + i, 4:8, :] = jnp.zeros((4, tokens), F32)

    send(0)
    send(1)
    mats(0)
    forward(0)
    send(2)

    @pl.loop(1, 4)
    def _(p):
        mats(p)

    forward(1)

    @pl.loop(0, 16)
    def _(t):
        st, j, h, p = where_at(t)

        @pl.when(t + 3 < 16)
        def _():
            send(t + 3)

        scatter(t)

        @pl.when(j >= 2)
        def _():
            ring(st, j - 2, range(0, SUBS // 2))

        @pl.when(t + 2 < 16)
        def _():
            forward(t + 2)

        @pl.when(j >= 2)
        def _():
            ring(st, j - 2, range(SUBS // 2, SUBS))

        @pl.when(j < 2)
        def _():
            for u in range(SUBS):
                for hh in range(2):

                    @pl.when(h == hh)
                    def _():
                        zcopy(st, hh, 0, u).start()

        @pl.when(t == 9)
        def _():
            finish(0, range(SUBS))

        @pl.when(t == 9)
        def _():
            @pl.loop(0, 4)
            def _(i):
                weights(i)

            dcopy(0).start()

        @pl.when(t >= 10)
        def _():
            s = t - 10
            dcopy(s).wait_recv()
            dacc[s + 2] += dland[s]
            dcopy(s + 1).start()

    finish(1, range(SUBS))
    dcopy(NZ - 2).wait_recv()
    dcomb_ref[...] = dacc[0] + dland[NZ - 2]

    @pl.loop(0, 2)
    def _(st):
        for h in range(2):

            @pl.loop(0, NZ - 1)
            def _(s):
                for u in range(SUBS):
                    zcopy(st, h, s, u).wait_send()

        @pl.loop(0, 8)
        def _(i):
            for k in range(3):
                xcopy(st, i // 4, i % 4, k, prod_ref).wait_send()
            fcopy(st, i // 4, i % 4).wait_send()

    @pl.loop(0, NZ - 1)
    def _(s):
        dcopy(s).wait_send()


def give_back(produced, d_rows, picked, meta, tokens, cap):
    features = 2 * produced.shape[3]
    hd = features // 2
    per = 2 * cap
    dma = pltpu.SemaphoreType.DMA
    vmem = pl.BlockSpec(memory_space=pltpu.VMEM)
    hbm = pl.BlockSpec(memory_space=pl.ANY)
    return pl.pallas_call(
        functools.partial(return_kernel, cap),
        out_shape=(
            jax.ShapeDtypeStruct((tokens, features), BF),
            jax.ShapeDtypeStruct((tokens, features), BF),
            jax.ShapeDtypeStruct((8, tokens), F32),
        ),
        in_specs=[hbm, hbm, vmem, vmem],
        out_specs=(vmem,) * 3,
        scratch_shapes=[
            pltpu.VMEM((2, 2, 4, 4 * per, hd), BF),
            pltpu.VMEM((2, 2, 4, per, hd), BF),
            pltpu.VMEM((2, 2, NZ * tokens, hd), BF),
            pltpu.VMEM((2, 2, NZ - 1, tokens, hd), BF),
            pltpu.VMEM((2, 4 * per, 2 * tokens), F32),
            pltpu.VMEM((2, 4, 2 * tokens, 4 * per), BF),
            pltpu.VMEM((NZ, 8, tokens), F32),
            pltpu.VMEM((NZ - 1, 8, tokens), F32),
            dma((2, 2, NZ - 1, SUBS)),
            dma((2, 2, NZ - 1, SUBS)),
            dma((NZ - 1,)),
            dma((NZ - 1,)),
            dma((2, 2, 4, 3)),
            dma((2, 2, 4, 3)),
            dma((2, 2, 4)),
            dma((2, 2, 4)),
            dma((2, 2, 4)),
        ],
        compiler_params=pltpu.CompilerParams(
            collective_id=1, has_side_effects=True, vmem_limit_bytes=62 * 1024 * 1024
        ),
        name="give_back",
    )(produced, d_rows, picked, meta)


def per_device(tokens, routes, combine, cotangent, w_gate, w_up, w_down):
    n, features = tokens.shape
    per_token = routes.shape[1]
    experts = w_gate.shape[0] * lax.axis_size("expert")
    cap = 3 * n * per_token // (2 * experts)
    per = 2 * cap
    rc = jnp.concatenate([routes.T.astype(F32), combine.T], axis=0)
    w_gate, w_up, w_down = w_gate[0], w_up[0], w_down[0]
    rows2, grad2, picked, meta, hid3, dga3, act3, produced = dispatch(
        tokens, cotangent, rc, w_gate, w_up, w_down, cap
    )

    def whole(a):
        return jnp.concatenate([a[0], a[1]], axis=-1).reshape(16 * per, features)

    def wide(a):
        return jnp.concatenate([a[0], a[1], a[2]], axis=-1)

    rows, d_in = whole(rows2), whole(grad2)
    hidden = wide(hid3)
    d_hidden = jnp.dot(d_in, w_down.T, preferred_element_type=F32)
    d_gate = (d_hidden * wide(dga3).astype(F32)).astype(BF)
    d_up = (d_hidden * wide(act3).astype(F32)).astype(BF)
    d_rows = (
        jnp.dot(d_gate, w_gate.T, preferred_element_type=F32)
        + jnp.dot(d_up, w_up.T, preferred_element_type=F32)
    ).astype(BF)
    d_rows = jnp.stack([d_rows[:, : features // 2], d_rows[:, features // 2 :]]).reshape(produced.shape)
    part_down = jnp.dot(hidden.T, d_in, preferred_element_type=F32).astype(BF)
    part_gate = jnp.dot(rows.T, d_gate, preferred_element_type=F32).astype(BF)
    part_up = jnp.dot(rows.T, d_up, preferred_element_type=F32).astype(BF)
    d_w_gate = lax.psum_scatter(part_gate[None], "dp", scatter_dimension=1, tiled=True)
    d_w_up = lax.psum_scatter(part_up[None], "dp", scatter_dimension=1, tiled=True)
    d_w_down = lax.psum_scatter(part_down[None], "dp", scatter_dimension=2, tiled=True)
    output, d_tokens, d_comb = give_back(produced, d_rows, picked, meta, n, cap)
    return output, d_tokens, d_comb[:per_token].T, d_w_gate, d_w_up, d_w_down


def solution(mesh):
    row = P(("dp", "expert"), None)
    weight = P("expert", None, None)
    return jax.shard_map(
        per_device,
        mesh=mesh,
        in_specs=(row, row, row, row, weight, weight, weight),
        out_specs=(
            row,
            row,
            row,
            P("expert", "dp", None),
            P("expert", "dp", None),
            P("expert", None, "dp"),
        ),
        check_vma=False,
    )
```

```python
import functools

import jax
import jax.numpy as jnp
from jax import lax
from jax.experimental import pallas as pl
from jax.experimental.pallas import tpu as pltpu
from jax.sharding import PartitionSpec as P

MESH = pl.DeviceIdType.MESH
NZ = 8
NX = 4
SUBS = 4
BF = jnp.bfloat16
F32 = jnp.float32


def neighbours():
    e = lax.axis_index("expert")
    x, z = e // NZ, e % NZ
    zp = x * NZ + (z + 1) % NZ
    zm = x * NZ + (z + NZ - 1) % NZ
    xp = ((x + 1) % NX) * NZ + z
    xm = ((x + NX - 1) % NX) * NZ + z
    return x, z, zp, zm, xp, xm


def greet(devices):
    barrier = pltpu.get_barrier_semaphore()
    for d in devices:
        pl.semaphore_signal(
            barrier, inc=1, device_id={"expert": d}, device_id_type=MESH
        )
    pl.semaphore_wait(barrier, len(devices))


def rcopy(src, dst, send, recv, dev):
    return pltpu.make_async_remote_copy(
        src_ref=src,
        dst_ref=dst,
        send_sem=send,
        recv_sem=recv,
        device_id={"expert": dev},
        device_id_type=MESH,
    )


def row_masks(meta, x, z, cap, blk):
    width = meta.shape[1]
    per = 2 * cap
    col = lax.broadcasted_iota(jnp.int32, (per, width), 1)
    row = lax.broadcasted_iota(jnp.int32, (per, width), 0)
    second = (row >= cap).astype(jnp.int32)
    shift = (col[0:1] >= width // 2).astype(jnp.int32) * 4096
    expert = ((x + blk + 1) % NX) * NZ + z
    ids = row - cap * second + 4096 * second + expert * cap
    return [ids == (meta[k : k + 1, :].astype(jnp.int32) + shift) for k in range(4)]


def dispatch_kernel(
    cap,
    tok_ref,
    cot_ref,
    rc_ref,
    wg_ref,
    wu_ref,
    wd_ref,
    rows_out,
    grad_out,
    picked_out,
    meta_out,
    hid_out,
    dga_out,
    act_out,
    prod_out,
    ag,
    metab,
    smat,
    cmat,
    sx,
    r,
    relay,
    wg,
    wu,
    wd,
    gate,
    hid,
    dga,
    act,
    prod,
    zs,
    zr,
    ms,
    mr,
    xs,
    xr,
    rs,
    rr,
    ls,
    ws,
    os_,
):
    tokens, features = tok_ref.shape
    ff = wg_ref.shape[1]
    hd = features // 2
    per = 2 * cap
    sub = tokens // SUBS
    ft = ff // 3
    nt = features // 4
    x, z, zp, zm, xp, xm = neighbours()
    zdev = (zp, zm)

    loads = []
    for st, src in enumerate((tok_ref, cot_ref)):
        for h in range(2):
            c = pltpu.make_async_copy(
                src.at[:, pl.ds(h * hd, hd)],
                ag.at[st, h, pl.ds(0, tokens), :],
                ls.at[st, h],
            )
            c.start()
            loads.append(c)

    def wload(i, f):
        if i == 2:
            return pltpu.make_async_copy(wd_ref.at[:, pl.ds(f * nt, nt)], wd.at[f], ws.at[i, f])
        src, dst = ((wg_ref, wg), (wu_ref, wu))[i]
        return pltpu.make_async_copy(src.at[:, pl.ds(f * ft, ft)], dst.at[f], ws.at[i, f])

    greet((zp, zm, xp, xm))

    def zcopy(st, h, s, u):
        a = s if h == 0 else (NZ - s) % NZ
        b = s + 1 if h == 0 else NZ - 1 - s
        src = ag.at[st, h, pl.ds(pl.multiple_of(a * tokens + sub * u, sub), sub), :]
        dst = ag.at[st, h, pl.ds(pl.multiple_of(b * tokens + sub * u, sub), sub), :]
        return rcopy(src, dst, zs.at[st, h, s, u], zr.at[st, h, s, u], zdev[h])

    def mcopy(h, s):
        a = s if h == 0 else (NZ - s) % NZ
        b = s + 1 if h == 0 else NZ - 1 - s
        return rcopy(metab.at[a], metab.at[b], ms.at[h, s], mr.at[h, s], zdev[h])

    def xcopy(st, h, p, i):
        far = jnp.where(h == 0, xp, xm)
        dst = relay.at[st, h, p] if i == 0 else r.at[st, h, p * 4 + i - 1]
        return rcopy(
            sx.at[st, h, p, pl.ds((1, 0, 2)[i] * per, per), :],
            dst,
            xs.at[st, h, p, i],
            xr.at[st, h, p, i],
            (far, xp, xm)[i],
        )

    def fcopy(st, h, p):
        far = jnp.where(h == 0, xp, xm)
        return rcopy(relay.at[st, h, p], r.at[st, h, p * 4 + 2], rs.at[st, h, p], rr.at[st, h, p], far)

    for h in range(2):
        loads[h].wait()
        for u in range(SUBS):
            zcopy(0, h, 0, u).start()
    for i, n in ((0, 3), (1, 3), (2, 4)):
        for f in range(n):
            wload(i, f).start()

    rc = rc_ref[...]
    experts = NX * NZ
    names = [rc[k : k + 1, :].astype(jnp.int32) for k in range(4)]
    ids = lax.broadcasted_iota(jnp.int32, (experts, tokens), 0)
    hits = [ids == n for n in names]
    count = sum(hit.astype(F32) for hit in hits)
    earlier = lax.broadcasted_iota(jnp.int32, (tokens, tokens), 0)
    later = lax.broadcasted_iota(jnp.int32, (tokens, tokens), 1)
    before = jnp.dot(
        count.astype(BF), (earlier < later).astype(F32).astype(BF), preferred_element_type=F32
    )
    for k in range(4):
        slot = jnp.sum(jnp.where(hits[k], before, 0.0), axis=0, keepdims=True)
        metab[0, k : k + 1, :] = rc[k : k + 1, :] * cap + slot
    metab[0, 4:8, :] = rc[4:8, :]
    for h in range(2):
        mcopy(h, 0).start()
    for c in loads[2:]:
        c.wait()

    def masks(p):
        meta = jnp.concatenate([metab[2 * p], metab[2 * p + 1]], axis=1)
        for blk in range(NX):
            hit = row_masks(meta, x, z, cap, blk)
            one = functools.reduce(jnp.logical_or, hit)
            weight = sum(jnp.where(hit[k], meta[4 + k : 5 + k, :], 0.0) for k in range(4))
            smat[p, blk * per : (blk + 1) * per, :] = one.astype(F32).astype(BF)
            cmat[p, blk * per : (blk + 1) * per, :] = jnp.broadcast_to(
                jnp.sum(weight, axis=1, keepdims=True), (per, 128)
            )

    def where_at(t):
        st, j = t // 8, t % 8
        h = j % 2
        return st, j, h, jnp.where(h == 0, j // 2, 3 - j // 2)

    def forward(t):
        st, _, h, p = where_at(t)
        xcopy(st, h, p, 0).wait_recv()
        fcopy(st, h, p).start()

    def arrived(st):
        @pl.loop(0, 8)
        def _(i):
            h, p = i // 4, i % 4
            for k in (1, 2):
                xcopy(st, h, p, k).wait_recv()
            fcopy(st, h, p).wait_recv()

    def project(w, f):
        a = jnp.dot(r[0, 0].reshape(-1, hd), w[f, 0:hd], preferred_element_type=F32)
        return a + jnp.dot(r[0, 1].reshape(-1, hd), w[f, hd:], preferred_element_type=F32)

    def gate_tile(f):
        gate[...] = project(wg, f)

    def up_tile(f):
        up = project(wu, f)
        g = gate[...]
        sig = 1.0 / (1.0 + jnp.exp(-g))
        a = g * sig
        act[f] = a.astype(BF)
        hid[f] = (a * up).astype(BF)
        dga[f] = (up * sig * (1.0 + g * (1.0 - sig))).astype(BF)

    def down_tile(h, part):
        n = 2 * h + part
        out = sum(
            jnp.dot(hid[f], wd[n, f * ft : (f + 1) * ft], preferred_element_type=F32)
            for f in range(3)
        )
        prod[h, :, :, part * nt : (part + 1) * nt] = out.astype(BF).reshape(16, per, nt)

    def ring(t, us):
        st, j, _, _ = where_at(t)

        @pl.when(j < NZ - 1)
        def _():
            for u in us:
                for h in range(2):
                    zcopy(st, h, j, u).wait_recv()

                    @pl.when(j < NZ - 2)
                    def _():
                        zcopy(st, h, j + 1, u).start()

                    @pl.when((j == NZ - 2) & (st == 0))
                    def _():
                        zcopy(1, h, 0, u).start()

    @pl.loop(0, 16)
    def _(t):
        st, j, h, p = where_at(t)

        @pl.when(st == 0)
        def _():
            for hh, n in ((0, 4), (1, 3)):

                @pl.when(j < n)
                def _():
                    mcopy(hh, j).wait_recv()

                @pl.when(j + 1 < n)
                def _():
                    mcopy(hh, j + 1).start()

        ring(t, range(0, SUBS // 2))

        @pl.when(t == 10)
        def _():
            arrived(0)
            for i, n in ((0, 3), (1, 3), (2, 4)):
                for f in range(n):
                    wload(i, f).wait()

        tile = (st == 1) & (j >= 2) & (j < 5)
        down = (st == 1) & (j >= 5) & (j < 7)

        @pl.when(tile)
        def _():
            gate_tile(j - 2)

        @pl.when(down)
        def _():
            down_tile(j - 5, 0)

        ring(t, range(SUBS // 2, SUBS))

        @pl.when(t > 0)
        def _():
            forward(t - 1)

        @pl.when(t < 4)
        def _():
            masks(p)

        got = jnp.dot(
            smat[p],
            ag[st, h, pl.ds(pl.multiple_of(p * 2 * tokens, 2 * tokens), 2 * tokens), :],
            preferred_element_type=F32,
        )
        got = (got * jnp.where(st == 1, cmat[p, :, 0:1], 1.0)).astype(BF)
        sx[st, h, p] = got
        r[st, h, p * 4 + 3] = got[3 * per :]
        for i in range(3):
            xcopy(st, h, p, i).start()

        @pl.when(tile)
        def _():
            up_tile(j - 2)

        @pl.when(down)
        def _():
            down_tile(j - 5, 1)

    outs = [(hid, hid_out), (dga, dga_out), (act, act_out), (prod, prod_out), (r.at[0], rows_out), (metab, meta_out), (sx.at[1], picked_out)]
    for i, (src, dst) in enumerate(outs):
        pltpu.make_async_copy(src, dst, os_.at[i]).start()
    forward(15)
    arrived(1)
    last = pltpu.make_async_copy(r.at[1], grad_out, os_.at[len(outs)])
    last.start()

    @pl.loop(0, 2)
    def _(st):
        for h in range(2):

            @pl.loop(0, NZ - 1)
            def _(s):
                for u in range(SUBS):
                    zcopy(st, h, s, u).wait_send()

        @pl.loop(0, 8)
        def _(i):
            for k in range(3):
                xcopy(st, i // 4, i % 4, k).wait_send()
            fcopy(st, i // 4, i % 4).wait_send()

    for h, n in ((0, 4), (1, 3)):
        for s in range(n):
            mcopy(h, s).wait_send()
    for i, (src, dst) in enumerate(outs):
        pltpu.make_async_copy(src, dst, os_.at[i]).wait()
    last.wait()


def dispatch(tokens, cotangent, rc, w_gate, w_up, w_down, cap):
    n, features = tokens.shape
    ff = w_gate.shape[1]
    hd = features // 2
    per = 2 * cap
    rows = 16 * per
    ft, nt = ff // 3, features // 4
    dma = pltpu.SemaphoreType.DMA
    vmem = pl.BlockSpec(memory_space=pltpu.VMEM)
    hbm = pl.BlockSpec(memory_space=pl.ANY)
    halves = jax.ShapeDtypeStruct((2, 16, per, hd), BF)
    hidden = jax.ShapeDtypeStruct((3, rows, ft), BF)
    return pl.pallas_call(
        functools.partial(dispatch_kernel, cap),
        out_shape=(
            halves,
            halves,
            jax.ShapeDtypeStruct((2, 4, 4 * per, hd), BF),
            jax.ShapeDtypeStruct((NZ, 8, n), F32),
            hidden,
            hidden,
            hidden,
            halves,
        ),
        in_specs=[hbm, hbm, vmem, hbm, hbm, hbm],
        out_specs=(hbm,) * 8,
        scratch_shapes=[
            pltpu.VMEM((2, 2, NZ * n, hd), BF),
            pltpu.VMEM((NZ, 8, n), F32),
            pltpu.VMEM((4, 4 * per, 2 * n), BF),
            pltpu.VMEM((4, 4 * per, 128), F32),
            pltpu.VMEM((2, 2, 4, 4 * per, hd), BF),
            pltpu.VMEM((2, 2, 16, per, hd), BF),
            pltpu.VMEM((2, 2, 4, per, hd), BF),
            pltpu.VMEM((3, features, ft), BF),
            pltpu.VMEM((3, features, ft), BF),
            pltpu.VMEM((4, ff, nt), BF),
            pltpu.VMEM((rows, ft), F32),
            pltpu.VMEM((3, rows, ft), BF),
            pltpu.VMEM((3, rows, ft), BF),
            pltpu.VMEM((3, rows, ft), BF),
            pltpu.VMEM((2, 16, per, hd), BF),
            dma((2, 2, NZ - 1, SUBS)),
            dma((2, 2, NZ - 1, SUBS)),
            dma((2, 4)),
            dma((2, 4)),
            dma((2, 2, 4, 3)),
            dma((2, 2, 4, 3)),
            dma((2, 2, 4)),
            dma((2, 2, 4)),
            dma((2, 2)),
            dma((3, 4)),
            dma((8,)),
        ],
        compiler_params=pltpu.CompilerParams(
            collective_id=0, has_side_effects=True, vmem_limit_bytes=62 * 1024 * 1024
        ),
        name="dispatch",
    )(tokens, cotangent, rc, w_gate, w_up, w_down)


def return_kernel(
    cap,
    prod_ref,
    rows_ref,
    grad_ref,
    picked_ref,
    hid_ref,
    dga_ref,
    act_ref,
    wg_ref,
    wu_ref,
    wd_ref,
    meta_ref,
    out_ref,
    dtok_ref,
    dcomb_ref,
    dwg_ref,
    dwu_ref,
    dwd_ref,
    q,
    relay,
    part,
    land,
    smat,
    stmat,
    dacc,
    dland,
    rows,
    grad,
    wd,
    hid,
    dga,
    act,
    big,
    drow,
    lc,
    ly,
    zs,
    zr,
    ds_,
    dr,
    xs,
    xr,
    rs,
    rr,
    ls,
    ws,
    cs,
    cr,
    ys,
    yr,
):
    tokens, features = out_ref.shape
    hd = features // 2
    per = 2 * cap
    sub = tokens // SUBS
    chunks, dch, ff = big.shape[1:]
    ft = ff // 3
    x, z, zp, zm, xp, xm = neighbours()
    zdev = (zp, zm)
    dp = lax.axis_index("dp")
    y, core = dp // 2, dp % 2
    ny = chunks // 2
    ydev = (((y + 1) % ny) * 2 + core, ((y + ny - 1) % ny) * 2 + core)
    partner = 2 * y + 1 - core

    loads = [
        (grad_ref, grad),
        (wd_ref.at[:, pl.ds(0, hd)], wd.at[0]),
        (wd_ref.at[:, pl.ds(hd, hd)], wd.at[1]),
        (dga_ref, dga),
        (act_ref, act),
        (wg_ref, big.at[0]),
        (wu_ref, big.at[1]),
        (rows_ref, rows),
        (hid_ref, hid),
        (picked_ref, wd),
    ]

    def load(i):
        return pltpu.make_async_copy(*loads[i], ws.at[i])

    for i in range(9):
        load(i).start()

    barrier = pltpu.get_barrier_semaphore()
    for d in (zp, zm, xp, xm):
        pl.semaphore_signal(barrier, inc=1, device_id={"expert": d}, device_id_type=MESH)
    for d in (partner, *ydev):
        pl.semaphore_signal(barrier, inc=1, device_id={"dp": d}, device_id_type=MESH)
    pl.semaphore_wait(barrier, 7)

    def where_at(t):
        st, j = t // 8, t % 8
        h = j % 2
        return st, j, h, jnp.where(h == 0, j // 2, 3 - j // 2)

    def xcopy(st, h, p, i, src):
        far = jnp.where(h == 0, xp, xm)
        dst = relay.at[st, h, p] if i == 0 else q.at[st, h, p, pl.ds((0, 2)[i - 1] * per, per), :]
        return rcopy(
            src.at[h, p * 4 + (2, 0, 1)[i]],
            dst,
            xs.at[st, h, p, i],
            xr.at[st, h, p, i],
            (far, xm, xp)[i],
        )

    def fcopy(st, h, p):
        far = jnp.where(h == 0, xp, xm)
        return rcopy(
            relay.at[st, h, p],
            q.at[st, h, p, pl.ds(per, per), :],
            rs.at[st, h, p],
            rr.at[st, h, p],
            far,
        )

    def own(st, h, p, src):
        return pltpu.make_async_copy(
            src.at[h, p * 4 + 3], q.at[st, h, p, pl.ds(3 * per, per), :], ls.at[st, h, p]
        )

    srcs = (prod_ref, drow)

    def send(t):
        st, _, h, p = where_at(t)
        for i in range(2):

            @pl.when(st == i)
            def _():
                for k in range(3):
                    xcopy(i, h, p, k, srcs[i]).start()
                own(i, h, p, srcs[i]).start()

    def forward(t):
        st, _, h, p = where_at(t)
        xcopy(st, h, p, 0, drow).wait_recv()
        fcopy(st, h, p).start()

    def chunk(h, s):
        return s + 1 if h == 0 else NZ - 1 - s

    def zcopy(st, h, s, u):
        m = chunk(h, s)
        src = part.at[st, h, pl.ds(pl.multiple_of(m * tokens + sub * u, sub), sub), :]
        dst = land.at[st, h, s, pl.ds(sub * u, sub), :]
        return rcopy(src, dst, zs.at[st, h, s, u], zr.at[st, h, s, u], zdev[h])

    def dcopy(s):
        return rcopy(dacc.at[s + 1], dland.at[s], ds_.at[s], dr.at[s], zp)

    def meta_of(p):
        return jnp.concatenate([meta_ref[2 * p], meta_ref[2 * p + 1]], axis=1)

    def mats(p):
        meta = meta_of(p)
        for blk in range(NX):
            hit = row_masks(meta, x, z, cap, blk)
            one = functools.reduce(jnp.logical_or, hit)
            weight = sum(jnp.where(hit[k], meta[4 + k : 5 + k, :], 0.0) for k in range(4))
            smat[0, blk * per : (blk + 1) * per, :] = weight
            smat[1, blk * per : (blk + 1) * per, :] = one.astype(F32)
        for i in range(2):
            stmat[i, p] = smat[i].T.astype(BF)

    def scatter(t):
        st, _, h, p = where_at(t)
        for k in (1, 2):
            xcopy(st, h, p, k, drow).wait_recv()
        fcopy(st, h, p).wait_recv()
        own(st, h, p, drow).wait()
        at = pl.ds(pl.multiple_of(p * 2 * tokens, 2 * tokens), 2 * tokens)
        part[st, h, at, :] = jnp.dot(
            stmat[st, p], q[st, h, p], preferred_element_type=F32
        ).astype(BF)

    def ring(st, s, us):
        for u in us:
            for h in range(2):
                m = chunk(h, s + 1)
                at = pl.ds(pl.multiple_of(m * tokens + sub * u, sub), sub)
                zcopy(st, h, s, u).wait_recv()
                part[st, h, at, :] += land[st, h, s, pl.ds(sub * u, sub), :]
                zcopy(st, h, s + 1, u).start()

    def finish(st, us):
        out = (out_ref, dtok_ref)[st]
        for u in us:
            at = pl.ds(sub * u, sub)
            for h in range(2):
                zcopy(st, h, NZ - 2, u).wait_recv()
                out[at, h * hd : (h + 1) * hd] = part[st, h, at, :] + land[st, h, NZ - 2, at, :]

    def weights(p):
        meta = meta_of(p)
        total = [jnp.zeros((1, 2 * tokens), F32)] * 4
        for blk in range(NX):
            v = jnp.zeros((per, 1), F32)
            for h in range(2):
                at = pl.ds(pl.multiple_of(p * 4 * per + blk * per, per), per)
                a = q[0, h, p, blk * per : (blk + 1) * per, :].astype(F32)
                b = wd[h, at, :].astype(F32)
                v = v + jnp.sum(a * b, axis=1, keepdims=True)
            hit = row_masks(meta, x, z, cap, blk)
            w = sum(jnp.where(hit[k], meta[4 + k : 5 + k, :], 0.0) for k in range(4))
            c = jnp.sum(w, axis=1, keepdims=True)
            v = v / jnp.where(c > 0.0, c, 1.0)
            for k in range(4):
                total[k] = total[k] + jnp.sum(jnp.where(hit[k], v, 0.0), axis=0, keepdims=True)
        for k in range(4):
            for i in range(2):
                dacc[2 * p + i, k : k + 1, :] = total[k][:, i * tokens : (i + 1) * tokens]
        for i in range(2):
            dacc[2 * p + i, 4:8, :] = jnp.zeros((4, tokens), F32)

    def nt(a, b):
        return lax.dot_general(a, b, (((1,), (1,)), ((), ())), preferred_element_type=F32)

    def hidden_tile(f):
        dh = nt(grad[0], wd[0, f * ft : (f + 1) * ft, :]) + nt(grad[1], wd[1, f * ft : (f + 1) * ft, :])
        dga[f] = (dh * dga[f].astype(F32)).astype(BF)
        act[f] = (dh * act[f].astype(F32)).astype(BF)

    def row_tile(n):
        out = sum(
            nt(dga[f], big[0, n, :, f * ft : (f + 1) * ft])
            + nt(act[f], big[1, n, :, f * ft : (f + 1) * ft])
            for f in range(3)
        )
        lanes = pl.ds(pl.multiple_of((n % 4) * dch, dch), dch)
        drow[n // 4, :, :, lanes] = out.astype(BF).reshape(16, per, dch)

    def target(k):
        return (y + jnp.where(k == 0, ny - 1, jnp.where(k == 3, 0, k))) % ny

    def grad_chunk(c):
        lanes = pl.ds(pl.multiple_of((c % 4) * dch, dch), dch)
        a = rows[c // 4, :, lanes].T
        b = grad[c // 4, :, lanes].T
        for i, (lhs, rhs) in enumerate(((a, dga), (a, act), (b, hid))):
            for f in range(3):
                big[i, c, :, f * ft : (f + 1) * ft] = jnp.dot(
                    lhs, rhs[f], preferred_element_type=F32
                ).astype(BF)

    def dpcopy(src, dst, send, recv, dev):
        return pltpu.make_async_remote_copy(
            src_ref=src,
            dst_ref=dst,
            send_sem=send,
            recv_sem=recv,
            device_id={"dp": dev},
            device_id_type=MESH,
        )

    def ccopy(k):
        return dpcopy(big.at[:, 2 * target(k) + 1 - core], lc.at[k], cs.at[k], cr.at[k], partner)

    half = dch // 2

    def ycopy(i, s, g):
        a = (y + 2 * ny - 1 - s) % ny if i == 0 else (y + 1 + s) % ny
        src = big.at[g, 2 * a + core, pl.ds(half * i, half), :]
        return dpcopy(src, ly.at[i, s, g], ys.at[i, s, g], yr.at[i, s, g], ydev[i])

    def grad_piece(k):
        mine = (k >= 4).astype(jnp.int32)
        kk = k - 4 * mine
        c = 2 * target(kk) + jnp.where(k >= 4, core, 1 - core)
        grad_chunk(c)

        @pl.when(k < 4)
        def _():
            ccopy(kk).start()

        @pl.when(k >= 4)
        def _():
            ccopy(kk).wait_recv()
            for i in range(3):
                big[i, c] += lc[kk, i]

            for i in range(2):

                @pl.when(kk == i)
                def _():
                    for g in range(3):
                        ycopy(i, 0, g).start()

    def dp_ring(n):
        s, g = n // 3, n % 3
        for i in range(2):
            b = (y + 2 * ny - 2 - s) % ny if i == 0 else (y + 2 + s) % ny
            ycopy(i, s, g).wait_recv()
            big[g, 2 * b + core, half * i : half * (i + 1), :] += ly[i, s, g]

            @pl.when(s < ny - 2)
            def _():
                ycopy(i, s + 1, g).start()

    def piece(slot):
        @pl.when(slot == 0)
        def _():
            hidden_tile(2)
            for i in (5, 6):
                load(i).wait()

        @pl.when((slot >= 1) & (slot < 9))
        def _():
            row_tile(slot - 1)

        @pl.when(slot == 2)
        def _():
            for i in (7, 8):
                load(i).wait()
            load(9).start()

        @pl.when((slot >= 9) & (slot < 17))
        def _():
            grad_piece(slot - 9)

        n = ((slot - 17) * 2 + 2) // 3

        @pl.when((slot >= 17) & (slot < 30) & ((slot - 17) % 3 != 2))
        def _():
            dp_ring(n)

    send(0)
    send(1)
    mats(0)
    for i in range(5):
        load(i).wait()
    hidden_tile(0)
    forward(0)
    send(2)
    mats(3)
    hidden_tile(1)
    forward(1)

    @pl.loop(0, 16)
    def _(t):
        st, j, h, p = where_at(t)

        @pl.when(t + 3 < 16)
        def _():
            send(t + 3)

        scatter(t)

        @pl.when(j < 2)
        def _():
            for u in range(SUBS):
                for hh in range(2):

                    @pl.when(h == hh)
                    def _():
                        zcopy(st, hh, 0, u).start()

        @pl.when(j >= 2)
        def _():
            ring(st, j - 2, range(0, SUBS // 2))

        @pl.when(t < 2)
        def _():
            mats(t + 1)

        piece(2 * t)

        @pl.when(t + 2 < 16)
        def _():
            forward(t + 2)

        @pl.when(j >= 2)
        def _():
            ring(st, j - 2, range(SUBS // 2, SUBS))

        piece(2 * t + 1)

        @pl.when(t == 9)
        def _():
            finish(0, range(SUBS))
            load(9).wait()

        @pl.when((t == 9) | (t == 10) | (t == 12) | (t == 14))
        def _():
            weights((t - 8) // 2)

        @pl.when(t == 9)
        def _():
            dcopy(0).start()

        @pl.when(t >= 10)
        def _():
            s = t - 10
            dcopy(s).wait_recv()
            dacc[s + 2] += dland[s]
            dcopy(s + 1).start()

    for g, out in enumerate((dwg_ref, dwu_ref)):
        out[...] = big[g, dp]
    dwd_ref[...] = big[2, dp].T
    finish(1, range(SUBS))
    dcopy(NZ - 2).wait_recv()
    dcomb_ref[...] = dacc[0] + dland[NZ - 2]

    @pl.loop(0, 2)
    def _(st):
        for h in range(2):

            @pl.loop(0, NZ - 1)
            def _(s):
                for u in range(SUBS):
                    zcopy(st, h, s, u).wait_send()

        @pl.loop(0, 8)
        def _(i):
            for k in range(3):
                xcopy(st, i // 4, i % 4, k, drow).wait_send()
            fcopy(st, i // 4, i % 4).wait_send()

    @pl.loop(0, NZ - 1)
    def _(s):
        dcopy(s).wait_send()

    @pl.loop(0, 4)
    def _(k):
        ccopy(k).wait_send()

    @pl.loop(0, 9)
    def _(n):
        for i in range(2):
            ycopy(i, n // 3, n % 3).wait_send()


def give_back(produced, rows, grad, picked, hid, dga, act, w_gate, w_up, w_down, meta, tokens, cap):
    features, ff = w_gate.shape
    hd = features // 2
    per = 2 * cap
    n_rows = 16 * per
    ndp = lax.axis_size("dp")
    dch = features // ndp
    ny = ndp // 2
    dma = pltpu.SemaphoreType.DMA
    vmem = pl.BlockSpec(memory_space=pltpu.VMEM)
    hbm = pl.BlockSpec(memory_space=pl.ANY)
    share = jax.ShapeDtypeStruct((dch, ff), BF)
    flat = (2, n_rows, hd)
    return pl.pallas_call(
        functools.partial(return_kernel, cap),
        out_shape=(
            jax.ShapeDtypeStruct((tokens, features), BF),
            jax.ShapeDtypeStruct((tokens, features), BF),
            jax.ShapeDtypeStruct((8, tokens), F32),
            share,
            share,
            jax.ShapeDtypeStruct((ff, dch), BF),
        ),
        in_specs=[hbm] * 10 + [vmem],
        out_specs=(vmem,) * 6,
        scratch_shapes=[
            pltpu.VMEM((2, 2, 4, 4 * per, hd), BF),
            pltpu.VMEM((2, 2, 4, per, hd), BF),
            pltpu.VMEM((2, 2, NZ * tokens, hd), BF),
            pltpu.VMEM((2, 2, NZ - 1, tokens, hd), BF),
            pltpu.VMEM((2, 4 * per, 2 * tokens), F32),
            pltpu.VMEM((2, 4, 2 * tokens, 4 * per), BF),
            pltpu.VMEM((NZ, 8, tokens), F32),
            pltpu.VMEM((NZ - 1, 8, tokens), F32),
            pltpu.VMEM(flat, BF),
            pltpu.VMEM(flat, BF),
            pltpu.VMEM((2, ff, hd), BF),
            pltpu.VMEM(hid.shape, BF),
            pltpu.VMEM(hid.shape, BF),
            pltpu.VMEM(hid.shape, BF),
            pltpu.VMEM((3, ndp, dch, ff), BF),
            pltpu.VMEM((2, 16, per, hd), BF),
            pltpu.VMEM((4, 3, dch, ff), BF),
            pltpu.VMEM((2, ny - 1, 3, dch // 2, ff), BF),
            dma((2, 2, NZ - 1, SUBS)),
            dma((2, 2, NZ - 1, SUBS)),
            dma((NZ - 1,)),
            dma((NZ - 1,)),
            dma((2, 2, 4, 3)),
            dma((2, 2, 4, 3)),
            dma((2, 2, 4)),
            dma((2, 2, 4)),
            dma((2, 2, 4)),
            dma((10,)),
            dma((4,)),
            dma((4,)),
            dma((2, ny - 1, 3)),
            dma((2, ny - 1, 3)),
        ],
        compiler_params=pltpu.CompilerParams(
            collective_id=1, has_side_effects=True, vmem_limit_bytes=67043328
        ),
        name="give_back",
    )(
        produced,
        rows.reshape(flat),
        grad.reshape(flat),
        picked.reshape(flat),
        hid,
        dga,
        act,
        w_gate.reshape(ndp, dch, ff),
        w_up.reshape(ndp, dch, ff),
        w_down,
        meta,
    )


def per_device(tokens, routes, combine, cotangent, w_gate, w_up, w_down):
    n = tokens.shape[0]
    per_token = routes.shape[1]
    experts = w_gate.shape[0] * lax.axis_size("expert")
    cap = 3 * n * per_token // (2 * experts)
    rc = jnp.concatenate([routes.T.astype(F32), combine.T], axis=0)
    w_gate, w_up, w_down = w_gate[0], w_up[0], w_down[0]
    rows, grad, picked, meta, hid, dga, act, produced = dispatch(
        tokens, cotangent, rc, w_gate, w_up, w_down, cap
    )
    output, d_tokens, d_comb, d_w_gate, d_w_up, d_w_down = give_back(
        produced, rows, grad, picked, hid, dga, act, w_gate, w_up, w_down, meta, n, cap
    )
    return output, d_tokens, d_comb[:per_token].T, d_w_gate[None], d_w_up[None], d_w_down[None]


def solution(mesh):
    row = P(("dp", "expert"), None)
    weight = P("expert", None, None)
    return jax.shard_map(
        per_device,
        mesh=mesh,
        in_specs=(row, row, row, row, weight, weight, weight),
        out_specs=(
            row,
            row,
            row,
            P("expert", "dp", None),
            P("expert", "dp", None),
            P("expert", None, "dp"),
        ),
        check_vma=False,
    )
```

```python
import functools

import jax
import jax.numpy as jnp
from jax import lax
from jax.experimental import pallas as pl
from jax.experimental.pallas import tpu as pltpu
from jax.sharding import PartitionSpec as P

MESH = pl.DeviceIdType.MESH
NZ = 8
NX = 4
SUBS = 4
BF = jnp.bfloat16
F32 = jnp.float32


def neighbours():
    e = lax.axis_index("expert")
    x, z = e // NZ, e % NZ
    zp = x * NZ + (z + 1) % NZ
    zm = x * NZ + (z + NZ - 1) % NZ
    xp = ((x + 1) % NX) * NZ + z
    xm = ((x + NX - 1) % NX) * NZ + z
    return x, z, zp, zm, xp, xm


def rcopy(src, dst, send, recv, dev):
    return pltpu.make_async_remote_copy(
        src_ref=src,
        dst_ref=dst,
        send_sem=send,
        recv_sem=recv,
        device_id={"expert": dev},
        device_id_type=MESH,
    )


def row_masks(meta, x, z, cap, blk):
    width = meta.shape[1]
    per = 2 * cap
    col = lax.broadcasted_iota(jnp.int32, (per, width), 1)
    row = lax.broadcasted_iota(jnp.int32, (per, width), 0)
    second = (row >= cap).astype(jnp.int32)
    shift = (col[0:1] >= width // 2).astype(jnp.int32) * 4096
    expert = ((x + blk + 1) % NX) * NZ + z
    ids = row - cap * second + 4096 * second + expert * cap
    return [ids == (meta[k : k + 1, :].astype(jnp.int32) + shift) for k in range(4)]


def layer_kernel(
    cap,
    tok_ref,
    cot_ref,
    routes_ref,
    combine_ref,
    wg_ref,
    wu_ref,
    wd_ref,
    out_ref,
    dtok_ref,
    dcomb_ref,
    dwg_ref,
    dwu_ref,
    dwd_ref,
    ag,
    sx,
    r,
    relay,
    q,
    land,
    big,
    wd,
    gate,
    hid,
    dga,
    act,
    prod,
    lc,
    ly,
    metab,
    smat,
    cmat,
    smatf,
    stmat,
    dacc,
    dland,
    zs,
    zr,
    ms,
    mr,
    xs,
    xr,
    rs,
    rr,
    ls,
    ws,
    os_,
    ds_,
    dr,
    cs,
    cr,
    ys,
    yr,
    free,
):
    tokens, features = tok_ref.shape
    ff = wg_ref.shape[1]
    hd = features // 2
    per = 2 * cap
    sub = tokens // SUBS
    ft, nt = ff // 3, features // 4
    x, z, zp, zm, xp, xm = neighbours()
    zdev = (zp, zm)
    dp = lax.axis_index("dp")
    y, core = dp // 2, dp % 2
    chunks = lax.axis_size("dp")
    ny = chunks // 2
    dch = features // chunks
    half = dch // 2
    ydev = (((y + 1) % ny) * 2 + core, ((y + ny - 1) % ny) * 2 + core)
    partner = 2 * y + 1 - core

    def rows_at(n, size):
        return pl.ds(pl.multiple_of(n * size, size), size)

    loads = [
        (tok_ref.at[:, pl.ds(0, hd)], ag.at[0, 0, pl.ds(0, tokens), :]),
        (tok_ref.at[:, pl.ds(hd, hd)], ag.at[0, 1, pl.ds(0, tokens), :]),
        (cot_ref.at[:, pl.ds(0, hd)], ag.at[1, 0, pl.ds(0, tokens), :]),
        (cot_ref.at[:, pl.ds(hd, hd)], ag.at[1, 1, pl.ds(0, tokens), :]),
        (wg_ref, big.at[0]),
        (wu_ref, big.at[1]),
        (wd_ref.at[:, pl.ds(0, hd)], wd.at[0]),
        (wd_ref.at[:, pl.ds(hd, hd)], wd.at[1]),
    ]

    def load(i):
        return pltpu.make_async_copy(*loads[i], ws.at[i])

    for i in range(4):
        load(i).start()

    barrier = pltpu.get_barrier_semaphore()
    for d in (zp, zm, xp, xm):
        pl.semaphore_signal(barrier, inc=1, device_id={"expert": d}, device_id_type=MESH)
    for d in (partner, *ydev):
        pl.semaphore_signal(barrier, inc=1, device_id={"dp": d}, device_id_type=MESH)
    pl.semaphore_wait(barrier, 7)

    def where_at(t):
        st, j = t // 8, t % 8
        h = j % 2
        return st, j, h, jnp.where(h == 0, j // 2, 3 - j // 2)


    def zout(st, h, s, u):
        a = s if h == 0 else (NZ - s) % NZ
        b = s + 1 if h == 0 else NZ - 1 - s
        src = ag.at[st, h, pl.ds(pl.multiple_of(a * tokens + sub * u, sub), sub), :]
        dst = ag.at[st, h, pl.ds(pl.multiple_of(b * tokens + sub * u, sub), sub), :]
        return rcopy(src, dst, zs.at[st, h, s, u], zr.at[st, h, s, u], zdev[h])

    def mcopy(h, s):
        a = s if h == 0 else (NZ - s) % NZ
        b = s + 1 if h == 0 else NZ - 1 - s
        return rcopy(metab.at[a], metab.at[b], ms.at[h, s], mr.at[h, s], zdev[h])

    def xout(st, h, p, i):
        far = jnp.where(h == 0, xp, xm)
        dst = relay.at[st, h, p] if i == 0 else r.at[st, h, rows_at(p * 4 + i - 1, per), :]
        return rcopy(
            sx.at[st, h, p, pl.ds((1, 0, 2)[i] * per, per), :],
            dst,
            xs.at[st, h, p, i],
            xr.at[st, h, p, i],
            (far, xp, xm)[i],
        )

    def fout(st, h, p):
        far = jnp.where(h == 0, xp, xm)
        return rcopy(
            relay.at[st, h, p],
            r.at[st, h, rows_at(p * 4 + 2, per), :],
            rs.at[st, h, p],
            rr.at[st, h, p],
            far,
        )


    def xback(st, h, p, i, src):
        far = jnp.where(h == 0, xp, xm)
        dst = relay.at[st, h, p] if i == 0 else q.at[st - 2, h, p, pl.ds((0, 2)[i - 1] * per, per), :]
        return rcopy(
            src.at[h, p, pl.ds((2, 0, 1)[i] * per, per), :],
            dst,
            xs.at[st, h, p, i],
            xr.at[st, h, p, i],
            (far, xm, xp)[i],
        )

    def fback(st, h, p):
        far = jnp.where(h == 0, xp, xm)
        return rcopy(
            relay.at[st, h, p],
            q.at[st - 2, h, p, pl.ds(per, per), :],
            rs.at[st, h, p],
            rr.at[st, h, p],
            far,
        )

    drow = sx.at[0]
    srcs = (prod, drow)

    def own(st, h, p, src):
        return pltpu.make_async_copy(
            src.at[h, p, pl.ds(3 * per, per), :],
            q.at[st - 2, h, p, pl.ds(3 * per, per), :],
            ls.at[st - 2, h, p],
        )

    def chunk(h, s):
        return s + 1 if h == 0 else NZ - 1 - s

    def zback(st, h, s, u):
        m = chunk(h, s)
        src = ag.at[st - 2, h, pl.ds(pl.multiple_of(m * tokens + sub * u, sub), sub), :]
        dst = land.at[h, s, pl.ds(sub * u, sub), :]
        return rcopy(src, dst, zs.at[st, h, s, u], zr.at[st, h, s, u], zdev[h])

    def dcopy(s):
        return rcopy(dacc.at[s + 1], dland.at[s], ds_.at[s], dr.at[s], zp)


    def dpcopy(src, dst, send, recv, dev):
        return pltpu.make_async_remote_copy(
            src_ref=src,
            dst_ref=dst,
            send_sem=send,
            recv_sem=recv,
            device_id={"dp": dev},
            device_id_type=MESH,
        )

    def target(k):
        return (y + jnp.where(k == 0, ny - 1, jnp.where(k == 3, 0, k))) % ny

    def ccopy(k):
        src = big.at[:, rows_at(2 * target(k) + 1 - core, dch), :]
        return dpcopy(src, lc.at[k], cs.at[k], cr.at[k], partner)

    def ycopy(i, s, g):
        a = (y + 2 * ny - 1 - s) % ny if i == 0 else (y + 1 + s) % ny
        src = big.at[g, rows_at(2 * (2 * a + core) + i, half), :]
        return dpcopy(src, ly.at[i, s, g], ys.at[i, s, g], yr.at[i, s, g], ydev[i])


    for h in range(2):
        load(h).wait()
        for u in range(SUBS):
            zout(0, h, 0, u).start()
    for i in range(4, 8):
        load(i).start()

    experts = NX * NZ
    names = [routes_ref[k : k + 1, :] for k in range(4)]
    ids = lax.broadcasted_iota(jnp.int32, (experts, tokens), 0)
    hits = [ids == n for n in names]
    count = sum(hit.astype(F32) for hit in hits)
    earlier = lax.broadcasted_iota(jnp.int32, (tokens, tokens), 0)
    later = lax.broadcasted_iota(jnp.int32, (tokens, tokens), 1)
    before = jnp.dot(
        count.astype(BF), (earlier < later).astype(F32).astype(BF), preferred_element_type=F32
    )
    for k in range(4):
        slot = jnp.sum(jnp.where(hits[k], before, 0.0), axis=0, keepdims=True)
        metab[0, k : k + 1, :] = names[k].astype(F32) * cap + slot
        metab[0, 4 + k : 5 + k, :] = combine_ref[k : k + 1, :]
    for h in range(2):
        mcopy(h, 0).start()
    for i in range(2, 4):
        load(i).wait()

    cmat[...] = jnp.zeros_like(cmat)

    def meta_of(p):
        return jnp.concatenate([metab[2 * p], metab[2 * p + 1]], axis=1)

    def masks(p):
        meta = meta_of(p)
        for blk in range(NX):
            at = pl.ds(blk * per, per)
            hit = row_masks(meta, x, z, cap, blk)
            one = functools.reduce(jnp.logical_or, hit).astype(F32)
            weight = sum(jnp.where(hit[k], meta[4 + k : 5 + k, :], 0.0) for k in range(4))
            smatf[at, :] = weight
            smat[p, at, :] = one.astype(BF)
            here = lax.broadcasted_iota(jnp.int32, (per, 128), 1) == p
            cmat[at, :] = jnp.where(here, jnp.sum(weight, axis=1, keepdims=True), cmat[at, :])
        stmat[0, p] = smatf[...].T.astype(BF)
        stmat[1, p] = smat[p].T

    def row_weights(p, at):
        size = cmat.shape[0] if at is None else per
        here = lax.broadcasted_iota(jnp.int32, (size, 128), 1) == p
        return jnp.sum(jnp.where(here, cmat[...] if at is None else cmat[at, :], 0.0), axis=1, keepdims=True)

    def forward_out(t):
        st, _, h, p = where_at(t)
        xout(st, h, p, 0).wait_recv()
        fout(st, h, p).start()

    def arrived(st):
        @pl.loop(0, 8)
        def _(i):
            h, p = i // 4, i % 4
            for k in (1, 2):
                xout(st, h, p, k).wait_recv()
            fout(st, h, p).wait_recv()

    def ring_out(t, u):
        st, j, _, _ = where_at(t)

        @pl.when(j < NZ - 1)
        def _():
            for h in range(2):
                zout(st, h, j, u).wait_recv()

                @pl.when(j < NZ - 2)
                def _():
                    zout(st, h, j + 1, u).start()

                @pl.when((j == NZ - 2) & (st == 0))
                def _():
                    zout(1, h, 0, u).start()

    def project(i, f):
        lanes = rows_at(f, ft)
        a = jnp.dot(r[0, 0], big[i, 0:hd, lanes], preferred_element_type=F32)
        return a + jnp.dot(r[0, 1], big[i, hd:, lanes], preferred_element_type=F32)

    def gate_tile(f):
        gate[...] = project(0, f)

    def up_tile(f):
        up = project(1, f)
        g = gate[...]
        sig = 1.0 / (1.0 + jnp.exp(-g))
        a = g * sig
        act[f] = a.astype(BF)
        hid[f] = (a * up).astype(BF)
        dga[f] = (up * sig * (1.0 + g * (1.0 - sig))).astype(BF)

    def down_tile(n):
        lanes = pl.ds((n % 2) * nt, nt)
        out = sum(
            jnp.dot(hid[f], wd[n // 2, f * ft : (f + 1) * ft, lanes], preferred_element_type=F32)
            for f in range(3)
        )
        prod[n // 2, :, :, lanes] = out.astype(BF).reshape(4, 4 * per, nt)

    def send(t):
        st, _, h, p = where_at(t)
        for i in range(2):

            @pl.when(st == i)
            def _():
                for k in range(3):
                    xback(2 + i, h, p, k, srcs[i]).start()
                own(2 + i, h, p, srcs[i]).start()

    def forward_back(t):
        st, _, h, p = where_at(t)
        xback(2 + st, h, p, 0, prod).wait_recv()
        fback(2 + st, h, p).start()

    @pl.loop(0, 16)
    def _(t):
        st, j, h, p = where_at(t)

        @pl.when(t == 14)
        def _():
            send(0)

        @pl.when(st == 0)
        def _():
            for hh, n in ((0, 4), (1, 3)):

                @pl.when(j < n)
                def _():
                    mcopy(hh, j).wait_recv()

                @pl.when(j + 1 < n)
                def _():
                    mcopy(hh, j + 1).start()

        for u in range(SUBS):
            ring_out(t, u)
            if u == 0:

                @pl.when(t == 10)
                def _():
                    arrived(0)
                    for i in range(4, 8):
                        load(i).wait()

                @pl.when((t >= 10) & (t < 13))
                def _():
                    gate_tile(t - 10)

            if u == 1:

                @pl.when(t > 0)
                def _():
                    forward_out(t - 1)

            if u == 2:

                @pl.when((t >= 10) & (t < 13))
                def _():
                    up_tile(t - 10)

            @pl.when(t == 13)
            def _():
                down_tile(u)

        @pl.when(t < 4)
        def _():
            masks(p)

        got = jnp.dot(
            smat[p], ag[st, h, rows_at(p, 2 * tokens), :], preferred_element_type=F32
        )
        got = (got * jnp.where(st == 1, row_weights(p, None), 1.0)).astype(BF)
        sx[st, h, p] = got
        r[st, h, rows_at(p * 4 + 3, per), :] = got[3 * per :]
        for i in range(3):
            xout(st, h, p, i).start()

        @pl.when(t == 15)
        def _():
            send(1)

    forward_out(15)
    forward_back(0)
    send(2)

    def sent_out(st):
        for h in range(2):

            @pl.loop(0, NZ - 1)
            def _(s):
                for u in range(SUBS):
                    zout(st, h, s, u).wait_send()

    def xsent_out(st):
        @pl.loop(0, 8)
        def _(i):
            for k in range(3):
                xout(st, i // 4, i % 4, k).wait_send()
            fout(st, i // 4, i % 4).wait_send()

    sent_out(0)
    xsent_out(0)
    forward_back(1)

    def scatter(t):
        st, _, h, p = where_at(t)
        for k in (1, 2):
            xback(2 + st, h, p, k, prod).wait_recv()
        fback(2 + st, h, p).wait_recv()
        own(2 + st, h, p, prod).wait()
        ag[st, h, rows_at(p, 2 * tokens), :] = jnp.dot(
            stmat[st, p], q[st, h, p], preferred_element_type=F32
        ).astype(BF)

    def upstream(h):
        return {"expert": zm if h == 0 else zp}

    def give_slot(h):
        pl.semaphore_signal(free.at[h], inc=1, device_id=upstream(h), device_id_type=MESH)

    def ring_back(st, s, u):
        for h in range(2):
            at = pl.ds(pl.multiple_of(chunk(h, s + 1) * tokens + sub * u, sub), sub)
            zback(2 + st, h, s, u).wait_recv()
            ag[st, h, at, :] += land[h, s, pl.ds(sub * u, sub), :]
            if u == 0:

                @pl.when(st == 1)
                def _():
                    pl.semaphore_wait(free.at[h], 1)

            zback(2 + st, h, s + 1, u).start()
            if u == SUBS - 1:

                @pl.when(st == 0)
                def _():
                    give_slot(h)

    def out_copy(st, h):
        return pltpu.make_async_copy(
            ag.at[st, h, pl.ds(0, tokens), :],
            (out_ref, dtok_ref)[st].at[:, pl.ds(h * hd, hd)],
            os_.at[st, h],
        )

    def finish(st):
        for h in range(2):
            for u in range(SUBS):
                zback(2 + st, h, NZ - 2, u).wait_recv()
            ag[st, h, 0:tokens, :] += land[h, NZ - 2]
            if st == 0:
                give_slot(h)
            out_copy(st, h).start()

    def weights(p):
        meta = meta_of(p)
        total = [jnp.zeros((1, 2 * tokens), F32)] * 4
        for blk in range(NX):
            at = pl.ds(blk * per, per)
            v = jnp.zeros((per, 1), F32)
            for h in range(2):
                v = v + jnp.sum(
                    q[0, h, p, at, :].astype(F32) * sx[1, h, p, at, :].astype(F32),
                    axis=1,
                    keepdims=True,
                )
            hit = row_masks(meta, x, z, cap, blk)
            c = row_weights(p, at)
            v = v / jnp.where(c > 0.0, c, 1.0)
            for k in range(4):
                total[k] = total[k] + jnp.sum(jnp.where(hit[k], v, 0.0), axis=0, keepdims=True)
        for i in range(2):
            for k in range(4):
                dacc[2 * p + i, k : k + 1, :] = total[k][:, i * tokens : (i + 1) * tokens]
            dacc[2 * p + i, 4:8, :] = jnp.zeros((4, tokens), F32)

    def nt_dot(a, b):
        return lax.dot_general(a, b, (((1,), (1,)), ((), ())), preferred_element_type=F32)

    def hidden_tile(f):
        at = rows_at(f, ft)
        dh = nt_dot(r[1, 0], wd[0, at, :]) + nt_dot(r[1, 1], wd[1, at, :])
        dga[f] = (dh * dga[f].astype(F32)).astype(BF)
        act[f] = (dh * act[f].astype(F32)).astype(BF)

    def row_tile(n):
        at = rows_at(n, dch)
        out = sum(
            nt_dot(dga[f], big[0, at, f * ft : (f + 1) * ft])
            + nt_dot(act[f], big[1, at, f * ft : (f + 1) * ft])
            for f in range(3)
        )
        each = chunks // 2
        sx[0, n // each, :, :, rows_at(n % each, dch)] = out.astype(BF).reshape(4, 4 * per, dch)

    def grad_chunk(c):
        each = chunks // 2
        lanes = rows_at(c % each, dch)
        a = r[0, c // each, :, lanes].T
        b = r[1, c // each, :, lanes].T
        for i, (lhs, rhs) in enumerate(((a, dga), (a, act), (b, hid))):
            for f in range(3):
                big[i, rows_at(c, dch), f * ft : (f + 1) * ft] = jnp.dot(
                    lhs, rhs[f], preferred_element_type=F32
                ).astype(BF)

    def grad_piece(k):
        mine = (k >= 4).astype(jnp.int32)
        kk = k - 4 * mine
        c = 2 * target(kk) + jnp.where(k >= 4, core, 1 - core)
        grad_chunk(c)

        @pl.when(k < 4)
        def _():
            ccopy(kk).start()

        @pl.when(k >= 4)
        def _():
            ccopy(kk).wait_recv()
            for i in range(3):
                big[i, rows_at(c, dch), :] += lc[kk, i]

            for i in range(2):

                @pl.when(kk == i)
                def _():
                    for g in range(3):
                        ycopy(i, 0, g).start()

    def dp_ring(n):
        s, g = n // 3, n % 3
        for i in range(2):
            b = (y + 2 * ny - 2 - s) % ny if i == 0 else (y + 2 + s) % ny
            ycopy(i, s, g).wait_recv()
            big[g, rows_at(2 * (2 * b + core) + i, half), :] += ly[i, s, g]

            @pl.when(s < ny - 2)
            def _():
                ycopy(i, s + 1, g).start()

    def piece(slot):
        @pl.when(slot == 10)
        def _():
            arrived(1)

        @pl.when((slot >= 10) & (slot < 16) & (slot % 2 == 0))
        def _():
            hidden_tile((slot - 10) // 2)

        @pl.when((slot >= 15) & (slot < 15 + chunks))
        def _():
            row_tile(slot - 15)

        @pl.when((slot >= 23) & (slot < 31))
        def _():
            grad_piece(slot - 23)

        @pl.when((slot >= 33) & (slot < 60) & (slot % 3 == 0))
        def _():
            dp_ring((slot - 33) // 3)

    @pl.loop(0, 16)
    def _(t):
        st, j, h, p = where_at(t)

        @pl.when(t + 3 < 16)
        def _():
            send(t + 3)

        @pl.when(t == 7)
        def _():
            sent_out(1)

        scatter(t)

        @pl.when(j < 2)
        def _():
            for hh in range(2):

                @pl.when(h == hh)
                def _():
                    @pl.when(st == 1)
                    def _():
                        pl.semaphore_wait(free.at[hh], 1)

                    for u in range(SUBS):
                        zback(2 + st, hh, 0, u).start()

        for u in range(SUBS):

            @pl.when(j >= 2)
            def _():
                ring_back(st, j - 2, u)

            piece(SUBS * t + u)
            if u == 1:

                @pl.when(t + 2 < 16)
                def _():
                    forward_back(t + 2)

        @pl.when(t == 9)
        def _():
            finish(0)

        @pl.when((t == 9) | (t == 10) | (t == 12) | (t == 14))
        def _():
            weights((t - 8) // 2)

        @pl.when(t == 9)
        def _():
            dcopy(0).start()

        @pl.when(t >= 10)
        def _():
            s = t - 10
            dcopy(s).wait_recv()
            dacc[s + 2] += dland[s]
            dcopy(s + 1).start()

    wd[0, :, 0:dch] = big[2, rows_at(dp, dch), :].T
    last = [
        pltpu.make_async_copy(big.at[0, rows_at(dp, dch), :], dwg_ref, os_.at[2, 0]),
        pltpu.make_async_copy(big.at[1, rows_at(dp, dch), :], dwu_ref, os_.at[2, 1]),
        pltpu.make_async_copy(wd.at[0, :, pl.ds(0, dch)], dwd_ref, os_.at[3, 0]),
    ]
    for c in last:
        c.start()
    finish(1)
    dcopy(NZ - 2).wait_recv()
    dcomb_ref[...] = dacc[0] + dland[NZ - 2]

    xsent_out(1)
    for h, n in ((0, 4), (1, 3)):
        for s in range(n):
            mcopy(h, s).wait_send()

    @pl.loop(2, 4)
    def _(st):
        for h in range(2):

            @pl.loop(0, NZ - 1)
            def _(s):
                for u in range(SUBS):
                    zback(st, h, s, u).wait_send()

        @pl.loop(0, 8)
        def _(i):
            for k in range(3):
                xback(st, i // 4, i % 4, k, prod).wait_send()
            fback(st, i // 4, i % 4).wait_send()

    @pl.loop(0, NZ - 1)
    def _(s):
        dcopy(s).wait_send()

    @pl.loop(0, 4)
    def _(k):
        ccopy(k).wait_send()

    @pl.loop(0, 9)
    def _(n):
        for i in range(2):
            ycopy(i, n // 3, n % 3).wait_send()

    for c in last:
        c.wait()
    for st in range(2):
        for h in range(2):
            out_copy(st, h).wait()


def layer(tokens, cotangent, routes, combine, w_gate, w_up, w_down, cap):
    n, features = tokens.shape
    ff = w_gate.shape[1]
    hd = features // 2
    per = 2 * cap
    rows = 16 * per
    ft = ff // 3
    ndp = lax.axis_size("dp")
    dch = features // ndp
    ny = ndp // 2
    dma = pltpu.SemaphoreType.DMA
    vmem = pl.BlockSpec(memory_space=pltpu.VMEM)
    hbm = pl.BlockSpec(memory_space=pl.ANY)
    share = jax.ShapeDtypeStruct((dch, ff), BF)
    full = jax.ShapeDtypeStruct((n, features), BF)
    return pl.pallas_call(
        functools.partial(layer_kernel, cap),
        out_shape=(
            full,
            full,
            jax.ShapeDtypeStruct((8, n), F32),
            share,
            share,
            jax.ShapeDtypeStruct((ff, dch), BF),
        ),
        in_specs=[hbm, hbm, vmem, vmem, hbm, hbm, hbm],
        out_specs=(hbm, hbm, vmem, hbm, hbm, hbm),
        scratch_shapes=[
            pltpu.VMEM((2, 2, NZ * n, hd), BF),
            pltpu.VMEM((2, 2, 4, 4 * per, hd), BF),
            pltpu.VMEM((2, 2, rows, hd), BF),
            pltpu.VMEM((4, 2, 4, per, hd), BF),
            pltpu.VMEM((2, 2, 4, 4 * per, hd), BF),
            pltpu.VMEM((2, NZ - 1, n, hd), BF),
            pltpu.VMEM((3, features, ff), BF),
            pltpu.VMEM((2, ff, hd), BF),
            pltpu.VMEM((rows, ft), F32),
            pltpu.VMEM((3, rows, ft), BF),
            pltpu.VMEM((3, rows, ft), BF),
            pltpu.VMEM((3, rows, ft), BF),
            pltpu.VMEM((2, 4, 4 * per, hd), BF),
            pltpu.VMEM((4, 3, dch, ff), BF),
            pltpu.VMEM((2, ny - 1, 3, dch // 2, ff), BF),
            pltpu.VMEM((NZ, 8, n), F32),
            pltpu.VMEM((4, 4 * per, 2 * n), BF),
            pltpu.VMEM((4 * per, 128), F32),
            pltpu.VMEM((4 * per, 2 * n), F32),
            pltpu.VMEM((2, 4, 2 * n, 4 * per), BF),
            pltpu.VMEM((NZ, 8, n), F32),
            pltpu.VMEM((NZ - 1, 8, n), F32),
            dma((4, 2, NZ - 1, SUBS)),
            dma((4, 2, NZ - 1, SUBS)),
            dma((2, 4)),
            dma((2, 4)),
            dma((4, 2, 4, 3)),
            dma((4, 2, 4, 3)),
            dma((4, 2, 4)),
            dma((4, 2, 4)),
            dma((2, 2, 4)),
            dma((8,)),
            dma((4, 2)),
            dma((NZ - 1,)),
            dma((NZ - 1,)),
            dma((4,)),
            dma((4,)),
            dma((2, ny - 1, 3)),
            dma((2, ny - 1, 3)),
            pltpu.SemaphoreType.REGULAR((2,)),
        ],
        compiler_params=pltpu.CompilerParams(
            collective_id=0, has_side_effects=True, vmem_limit_bytes=67043328
        ),
        name="layer",
    )(tokens, cotangent, routes, combine, w_gate, w_up, w_down)


def close_kernel(*refs):
    n = len(refs) // 2
    for src, dst in zip(refs[:n], refs[n:]):
        dst[...] = src[: dst.shape[0]]


def close(arrays, top):
    vmem = pl.BlockSpec(memory_space=pltpu.VMEM)
    shapes = [jax.ShapeDtypeStruct(a.shape, a.dtype) for a in arrays]
    shapes[2] = jax.ShapeDtypeStruct((top, arrays[2].shape[1]), F32)
    return pl.pallas_call(
        close_kernel,
        out_shape=tuple(shapes),
        in_specs=[vmem] * len(arrays),
        out_specs=(vmem,) * len(arrays),
        name="close",
    )(*arrays)


def per_device(tokens, routes, combine, cotangent, w_gate, w_up, w_down):
    n = tokens.shape[0]
    per_token = routes.shape[1]
    experts = w_gate.shape[0] * lax.axis_size("expert")
    cap = 3 * n * per_token // (2 * experts)
    arrays = layer(
        tokens, cotangent, routes.T, combine.T, w_gate[0], w_up[0], w_down[0], cap
    )
    output, d_tokens, d_comb, d_w_gate, d_w_up, d_w_down = close(arrays, per_token)
    return output, d_tokens, d_comb.T, d_w_gate[None], d_w_up[None], d_w_down[None]


def solution(mesh):
    row = P(("dp", "expert"), None)
    weight = P("expert", None, None)
    return jax.shard_map(
        per_device,
        mesh=mesh,
        in_specs=(row, row, row, row, weight, weight, weight),
        out_specs=(
            row,
            row,
            row,
            P("expert", "dp", None),
            P("expert", "dp", None),
            P("expert", None, "dp"),
        ),
        check_vma=False,
    )
```

```python
import functools

import jax
import jax.numpy as jnp
from jax import lax
from jax.experimental import pallas as pl
from jax.experimental.pallas import tpu as pltpu
from jax.sharding import PartitionSpec as P

MESH = pl.DeviceIdType.MESH
NZ = 8
NX = 4
FOUT = 0
LATE = 2
PAIR = 30
RING = 36
AHEAD = 3
SUBS = 4
BF = jnp.bfloat16
F32 = jnp.float32


def neighbours():
    e = lax.axis_index("expert")
    x, z = e // NZ, e % NZ
    zp = x * NZ + (z + 1) % NZ
    zm = x * NZ + (z + NZ - 1) % NZ
    xp = ((x + 1) % NX) * NZ + z
    xm = ((x + NX - 1) % NX) * NZ + z
    return x, z, zp, zm, xp, xm


def rcopy(src, dst, send, recv, dev):
    return pltpu.make_async_remote_copy(
        src_ref=src,
        dst_ref=dst,
        send_sem=send,
        recv_sem=recv,
        device_id={"expert": dev},
        device_id_type=MESH,
    )


def row_masks(meta, x, z, cap, blk):
    width = meta.shape[1]
    per = 2 * cap
    col = lax.broadcasted_iota(jnp.int32, (per, width), 1)
    row = lax.broadcasted_iota(jnp.int32, (per, width), 0)
    second = (row >= cap).astype(jnp.int32)
    shift = (col[0:1] >= width // 2).astype(jnp.int32) * 4096
    expert = ((x + blk + 1) % NX) * NZ + z
    ids = row - cap * second + 4096 * second + expert * cap
    return [ids == (meta[k : k + 1, :].astype(jnp.int32) + shift) for k in range(4)]


def layer_kernel(
    cap,
    tok_ref,
    cot_ref,
    routes_ref,
    combine_ref,
    wg_ref,
    wu_ref,
    wd_ref,
    out_ref,
    dtok_ref,
    dcomb_ref,
    dwg_ref,
    dwu_ref,
    dwd_ref,
    ag,
    sx,
    r,
    relay,
    q,
    land,
    big,
    wd,
    gate,
    hid,
    dga,
    act,
    prod,
    lc,
    ly,
    metab,
    smat,
    cmat,
    smatf,
    stmat,
    dacc,
    dland,
    zs,
    zr,
    ms,
    mr,
    xs,
    xr,
    rs,
    rr,
    ls,
    ws,
    os_,
    ds_,
    dr,
    cs,
    cr,
    ys,
    yr,
    free,
):
    tokens, features = tok_ref.shape
    ff = wg_ref.shape[1]
    hd = features // 2
    per = 2 * cap
    sub = tokens // SUBS
    ft, nt = ff // 3, features // 4
    x, z, zp, zm, xp, xm = neighbours()
    zdev = (zp, zm)
    dp = lax.axis_index("dp")
    y, core = dp // 2, dp % 2
    chunks = lax.axis_size("dp")
    ny = chunks // 2
    dch = features // chunks
    half = dch // 2
    ydev = (((y + 1) % ny) * 2 + core, ((y + ny - 1) % ny) * 2 + core)
    partner = 2 * y + 1 - core

    def rows_at(n, size):
        return pl.ds(pl.multiple_of(n * size, size), size)

    loads = [
        (tok_ref.at[:, pl.ds(0, hd)], ag.at[0, 0, pl.ds(0, tokens), :]),
        (tok_ref.at[:, pl.ds(hd, hd)], ag.at[0, 1, pl.ds(0, tokens), :]),
        (cot_ref.at[:, pl.ds(0, hd)], ag.at[1, 0, pl.ds(0, tokens), :]),
        (cot_ref.at[:, pl.ds(hd, hd)], ag.at[1, 1, pl.ds(0, tokens), :]),
        (wg_ref, big.at[0]),
        (wu_ref, big.at[1]),
        (wd_ref.at[:, pl.ds(0, hd)], wd.at[0]),
        (wd_ref.at[:, pl.ds(hd, hd)], wd.at[1]),
    ]

    def load(i):
        return pltpu.make_async_copy(*loads[i], ws.at[i])

    for i in range(4):
        load(i).start()

    barrier = pltpu.get_barrier_semaphore()
    for d in (zp, zm, xp, xm):
        pl.semaphore_signal(barrier, inc=1, device_id={"expert": d}, device_id_type=MESH)
    for d in (partner, *ydev):
        pl.semaphore_signal(barrier, inc=1, device_id={"dp": d}, device_id_type=MESH)
    pl.semaphore_wait(barrier, 7)

    def where_at(t):
        st, j = t // 8, t % 8
        h = j % 2
        return st, j, h, jnp.where(h == 0, j // 2, 3 - j // 2)


    def zout(st, h, s, u):
        a = s if h == 0 else (NZ - s) % NZ
        b = s + 1 if h == 0 else NZ - 1 - s
        src = ag.at[st, h, pl.ds(pl.multiple_of(a * tokens + sub * u, sub), sub), :]
        dst = ag.at[st, h, pl.ds(pl.multiple_of(b * tokens + sub * u, sub), sub), :]
        return rcopy(src, dst, zs.at[st, h, s, u], zr.at[st, h, s, u], zdev[h])

    def mcopy(h, s):
        a = s if h == 0 else (NZ - s) % NZ
        b = s + 1 if h == 0 else NZ - 1 - s
        return rcopy(metab.at[a], metab.at[b], ms.at[h, s], mr.at[h, s], zdev[h])

    def xout(st, h, p, i):
        far = jnp.where(h == 0, xp, xm)
        dst = relay.at[st, h, p] if i == 0 else r.at[st, h, rows_at(p * 4 + i - 1, per), :]
        return rcopy(
            sx.at[st, h, p, pl.ds((1, 0, 2)[i] * per, per), :],
            dst,
            xs.at[st, h, p, i],
            xr.at[st, h, p, i],
            (far, xp, xm)[i],
        )

    def fout(st, h, p):
        far = jnp.where(h == 0, xp, xm)
        return rcopy(
            relay.at[st, h, p],
            r.at[st, h, rows_at(p * 4 + 2, per), :],
            rs.at[st, h, p],
            rr.at[st, h, p],
            far,
        )


    def xback(st, h, p, i, src):
        far = jnp.where(h == 0, xp, xm)
        dst = relay.at[st, h, p] if i == 0 else q.at[st - 2, h, p, pl.ds((0, 2)[i - 1] * per, per), :]
        return rcopy(
            src.at[h, p, pl.ds((2, 0, 1)[i] * per, per), :],
            dst,
            xs.at[st, h, p, i],
            xr.at[st, h, p, i],
            (far, xm, xp)[i],
        )

    def fback(st, h, p):
        far = jnp.where(h == 0, xp, xm)
        return rcopy(
            relay.at[st, h, p],
            q.at[st - 2, h, p, pl.ds(per, per), :],
            rs.at[st, h, p],
            rr.at[st, h, p],
            far,
        )

    drow = sx.at[0]
    srcs = (prod, drow)

    def own(st, h, p, src):
        return pltpu.make_async_copy(
            src.at[h, p, pl.ds(3 * per, per), :],
            q.at[st - 2, h, p, pl.ds(3 * per, per), :],
            ls.at[st - 2, h, p],
        )

    def chunk(h, s):
        return s + 1 if h == 0 else NZ - 1 - s

    def zback(st, h, s, u):
        m = chunk(h, s)
        src = ag.at[st - 2, h, pl.ds(pl.multiple_of(m * tokens + sub * u, sub), sub), :]
        dst = land.at[h, s, pl.ds(sub * u, sub), :]
        return rcopy(src, dst, zs.at[st, h, s, u], zr.at[st, h, s, u], zdev[h])

    def dcopy(s):
        return rcopy(dacc.at[s + 1], dland.at[s], ds_.at[s], dr.at[s], zp)


    def dpcopy(src, dst, send, recv, dev):
        return pltpu.make_async_remote_copy(
            src_ref=src,
            dst_ref=dst,
            send_sem=send,
            recv_sem=recv,
            device_id={"dp": dev},
            device_id_type=MESH,
        )

    def target(k):
        return (y + jnp.where(k == 0, ny - 1, jnp.where(k == 3, 0, k))) % ny

    def ccopy(k):
        src = big.at[:, rows_at(2 * target(k) + 1 - core, dch), :]
        return dpcopy(src, lc.at[k], cs.at[k], cr.at[k], partner)

    def ycopy(i, s, g):
        a = (y + 2 * ny - 1 - s) % ny if i == 0 else (y + 1 + s) % ny
        src = big.at[g, rows_at(2 * (2 * a + core) + i, half), :]
        return dpcopy(src, ly.at[i, s, g], ys.at[i, s, g], yr.at[i, s, g], ydev[i])


    for h in range(2):
        load(h).wait()
        for u in range(SUBS):
            zout(0, h, 0, u).start()
    for i in range(4, 8):
        load(i).start()

    experts = NX * NZ
    names = [routes_ref[k : k + 1, :] for k in range(4)]
    ids = lax.broadcasted_iota(jnp.int32, (experts, tokens), 0)
    hits = [ids == n for n in names]
    count = sum(hit.astype(F32) for hit in hits)
    earlier = lax.broadcasted_iota(jnp.int32, (tokens, tokens), 0)
    later = lax.broadcasted_iota(jnp.int32, (tokens, tokens), 1)
    before = jnp.dot(
        count.astype(BF), (earlier < later).astype(F32).astype(BF), preferred_element_type=F32
    )
    for k in range(4):
        slot = jnp.sum(jnp.where(hits[k], before, 0.0), axis=0, keepdims=True)
        metab[0, k : k + 1, :] = names[k].astype(F32) * cap + slot
        metab[0, 4 + k : 5 + k, :] = combine_ref[k : k + 1, :]
    for h in range(2):
        mcopy(h, 0).start()
    for i in range(2, 4):
        load(i).wait()

    cmat[...] = jnp.zeros_like(cmat)

    def meta_of(p):
        return jnp.concatenate([metab[2 * p], metab[2 * p + 1]], axis=1)

    def masks(p):
        meta = meta_of(p)
        for blk in range(NX):
            at = pl.ds(blk * per, per)
            hit = row_masks(meta, x, z, cap, blk)
            one = functools.reduce(jnp.logical_or, hit).astype(F32)
            weight = sum(jnp.where(hit[k], meta[4 + k : 5 + k, :], 0.0) for k in range(4))
            smatf[at, :] = weight
            smat[p, at, :] = one.astype(BF)
            here = lax.broadcasted_iota(jnp.int32, (per, 128), 1) == p
            cmat[at, :] = jnp.where(here, jnp.sum(weight, axis=1, keepdims=True), cmat[at, :])
        stmat[0, p] = smatf[...].T.astype(BF)
        stmat[1, p] = smat[p].T

    def row_weights(p, at):
        size = cmat.shape[0] if at is None else per
        here = lax.broadcasted_iota(jnp.int32, (size, 128), 1) == p
        return jnp.sum(jnp.where(here, cmat[...] if at is None else cmat[at, :], 0.0), axis=1, keepdims=True)

    def forward_out(t):
        st, _, h, p = where_at(t)
        xout(st, h, p, 0).wait_recv()
        fout(st, h, p).start()

    def arrived(st):
        @pl.loop(0, 8)
        def _(i):
            h, p = i // 4, i % 4
            for k in (1, 2):
                xout(st, h, p, k).wait_recv()
            fout(st, h, p).wait_recv()

    def ring_out(t, u):
        st, j, _, _ = where_at(t)

        @pl.when(j < NZ - 1)
        def _():
            for h in range(2):
                zout(st, h, j, u).wait_recv()

                @pl.when(j < NZ - 2)
                def _():
                    zout(st, h, j + 1, u).start()

                @pl.when((j == NZ - 2) & (st == 0))
                def _():
                    zout(1, h, 0, u).start()

    def project(i, f):
        lanes = rows_at(f, ft)
        a = jnp.dot(r[0, 0], big[i, 0:hd, lanes], preferred_element_type=F32)
        return a + jnp.dot(r[0, 1], big[i, hd:, lanes], preferred_element_type=F32)

    def gate_tile(f):
        gate[...] = project(0, f)

    def up_tile(f):
        up = project(1, f)
        g = gate[...]
        sig = 1.0 / (1.0 + jnp.exp(-g))
        a = g * sig
        act[f] = a.astype(BF)
        hid[f] = (a * up).astype(BF)
        dga[f] = (up * sig * (1.0 + g * (1.0 - sig))).astype(BF)

    def down_tile(n):
        lanes = pl.ds((n % 2) * nt, nt)
        out = sum(
            jnp.dot(hid[f], wd[n // 2, f * ft : (f + 1) * ft, lanes], preferred_element_type=F32)
            for f in range(3)
        )
        prod[n // 2, :, :, lanes] = out.astype(BF).reshape(4, 4 * per, nt)

    def send(t):
        st, _, h, p = where_at(t)
        for i in range(2):

            @pl.when(st == i)
            def _():
                for k in range(3):
                    xback(2 + i, h, p, k, srcs[i]).start()
                own(2 + i, h, p, srcs[i]).start()

    def forward_back(t):
        st, _, h, p = where_at(t)
        xback(2 + st, h, p, 0, prod).wait_recv()
        fback(2 + st, h, p).start()

    @pl.loop(0, 16)
    def _(t):
        st, j, h, p = where_at(t)

        for i in range(2):

            @pl.when(t == 13 + i)
            def _():
                send(i)

        @pl.when(st == 0)
        def _():
            for hh, n in ((0, 4), (1, 3)):

                @pl.when(j < n)
                def _():
                    mcopy(hh, j).wait_recv()

                @pl.when(j + 1 < n)
                def _():
                    mcopy(hh, j + 1).start()

        for u in range(SUBS):
            ring_out(t, u)
            if u == 0:

                @pl.when(t == 10)
                def _():
                    arrived(0)
                    for i in range(4, 8):
                        load(i).wait()

            slot = SUBS * (t - 10) + u

            @pl.when((slot >= 0) & (slot < 6))
            def _():
                if u % 2 == 0:
                    gate_tile(slot // 2)
                else:
                    up_tile(slot // 2)

            for i in range(4):
                if (6 + i) % SUBS == u:

                    @pl.when(slot == 6 + i)
                    def _():
                        down_tile(i)

            if u == FOUT:

                @pl.when(t >= LATE)
                def _():
                    forward_out(t - LATE)

            if u == 1:

                @pl.when(t == 15)
                def _():
                    forward_back(0)

        @pl.when(t < 4)
        def _():
            masks(p)

        got = jnp.dot(
            smat[p], ag[st, h, rows_at(p, 2 * tokens), :], preferred_element_type=F32
        )
        got = (got * jnp.where(st == 1, row_weights(p, None), 1.0)).astype(BF)
        sx[st, h, p] = got
        r[st, h, rows_at(p * 4 + 3, per), :] = got[3 * per :]
        for i in range(3):
            xout(st, h, p, i).start()

    for i in range(LATE):
        forward_out(16 - LATE + i)
    for i in range(2, AHEAD):
        send(i)

    def sent_out(st):
        for h in range(2):

            @pl.loop(0, NZ - 1)
            def _(s):
                for u in range(SUBS):
                    zout(st, h, s, u).wait_send()

    def xsent_out(st):
        @pl.loop(0, 8)
        def _(i):
            for k in range(3):
                xout(st, i // 4, i % 4, k).wait_send()
            fout(st, i // 4, i % 4).wait_send()

    sent_out(0)
    xsent_out(0)
    for i in range(1, AHEAD - 1):
        forward_back(i)

    def scatter(t):
        st, _, h, p = where_at(t)
        for k in (1, 2):
            xback(2 + st, h, p, k, prod).wait_recv()
        fback(2 + st, h, p).wait_recv()
        own(2 + st, h, p, prod).wait()
        ag[st, h, rows_at(p, 2 * tokens), :] = jnp.dot(
            stmat[st, p], q[st, h, p], preferred_element_type=F32
        ).astype(BF)

    def upstream(h):
        return {"expert": zm if h == 0 else zp}

    def give_slot(h):
        pl.semaphore_signal(free.at[h], inc=1, device_id=upstream(h), device_id_type=MESH)

    def ring_back(st, s, u):
        for h in range(2):
            at = pl.ds(pl.multiple_of(chunk(h, s + 1) * tokens + sub * u, sub), sub)
            zback(2 + st, h, s, u).wait_recv()
            ag[st, h, at, :] += land[h, s, pl.ds(sub * u, sub), :]
            if u == 0:

                @pl.when(st == 1)
                def _():
                    pl.semaphore_wait(free.at[h], 1)

            zback(2 + st, h, s + 1, u).start()
            if u == SUBS - 1:

                @pl.when(st == 0)
                def _():
                    give_slot(h)

    def out_copy(st, h):
        return pltpu.make_async_copy(
            ag.at[st, h, pl.ds(0, tokens), :],
            (out_ref, dtok_ref)[st].at[:, pl.ds(h * hd, hd)],
            os_.at[st, h],
        )

    def finish(st):
        for h in range(2):
            for u in range(SUBS):
                zback(2 + st, h, NZ - 2, u).wait_recv()
            ag[st, h, 0:tokens, :] += land[h, NZ - 2]
            if st == 0:
                give_slot(h)
            out_copy(st, h).start()

    def weights(p):
        meta = meta_of(p)
        total = [jnp.zeros((1, 2 * tokens), F32)] * 4
        for blk in range(NX):
            at = pl.ds(blk * per, per)
            v = jnp.zeros((per, 1), F32)
            for h in range(2):
                v = v + jnp.sum(
                    q[0, h, p, at, :].astype(F32) * sx[1, h, p, at, :].astype(F32),
                    axis=1,
                    keepdims=True,
                )
            hit = row_masks(meta, x, z, cap, blk)
            c = row_weights(p, at)
            v = v / jnp.where(c > 0.0, c, 1.0)
            for k in range(4):
                total[k] = total[k] + jnp.sum(jnp.where(hit[k], v, 0.0), axis=0, keepdims=True)
        for i in range(2):
            for k in range(4):
                dacc[2 * p + i, k : k + 1, :] = total[k][:, i * tokens : (i + 1) * tokens]
            dacc[2 * p + i, 4:8, :] = jnp.zeros((4, tokens), F32)

    def nt_dot(a, b):
        return lax.dot_general(a, b, (((1,), (1,)), ((), ())), preferred_element_type=F32)

    def hidden_first(f):
        gate[...] = nt_dot(r[1, 0], wd[0, rows_at(f, ft), :])

    def hidden_second(f):
        dh = gate[...] + nt_dot(r[1, 1], wd[1, rows_at(f, ft), :])
        dga[f] = (dh * dga[f].astype(F32)).astype(BF)
        act[f] = (dh * act[f].astype(F32)).astype(BF)

    def row_tile(n):
        at = rows_at(n, dch)
        out = sum(
            nt_dot(dga[f], big[0, at, f * ft : (f + 1) * ft])
            + nt_dot(act[f], big[1, at, f * ft : (f + 1) * ft])
            for f in range(3)
        )
        each = chunks // 2
        sx[0, n // each, :, :, rows_at(n % each, dch)] = out.astype(BF).reshape(4, 4 * per, dch)

    def grad_chunk(c):
        each = chunks // 2
        lanes = rows_at(c % each, dch)
        a = r[0, c // each, :, lanes].T
        b = r[1, c // each, :, lanes].T
        for i, (lhs, rhs) in enumerate(((a, dga), (a, act), (b, hid))):
            for f in range(3):
                big[i, rows_at(c, dch), f * ft : (f + 1) * ft] = jnp.dot(
                    lhs, rhs[f], preferred_element_type=F32
                ).astype(BF)

    def grad_piece(k):
        kk = k % 4
        grad_chunk(2 * target(kk) + jnp.where(k >= 4, core, 1 - core))

        @pl.when(k < 4)
        def _():
            ccopy(kk).start()

    def pair_sum(k):
        at = rows_at(2 * target(k) + core, dch)
        ccopy(k).wait_recv()
        for i in range(3):
            big[i, at, :] += lc[k, i]

        for i in range(2):

            @pl.when(k == i)
            def _():
                for g in range(3):
                    ycopy(i, 0, g).start()

    def dp_ring(n):
        s, g = n // 3, n % 3
        for i in range(2):
            b = (y + 2 * ny - 2 - s) % ny if i == 0 else (y + 2 + s) % ny
            ycopy(i, s, g).wait_recv()
            big[g, rows_at(2 * (2 * b + core) + i, half), :] += ly[i, s, g]

            @pl.when(s < ny - 2)
            def _():
                ycopy(i, s + 1, g).start()

    def piece(slot):
        @pl.when(slot == 10)
        def _():
            arrived(1)

        @pl.when((slot >= 10) & (slot < 16))
        def _():
            @pl.when(slot % 2 == 0)
            def _():
                hidden_first((slot - 10) // 2)

            @pl.when(slot % 2 == 1)
            def _():
                hidden_second((slot - 10) // 2)

        @pl.when((slot >= 16) & (slot < 16 + chunks))
        def _():
            row_tile(slot - 16)

        @pl.when((slot >= 24) & (slot < 32))
        def _():
            grad_piece(slot - 24)

        @pl.when((slot >= PAIR) & (slot < PAIR + 4))
        def _():
            pair_sum(slot - PAIR)

        @pl.when((slot >= RING) & (slot < RING + 27) & ((slot - RING) % 3 == 0))
        def _():
            dp_ring((slot - RING) // 3)

    @pl.loop(0, 16)
    def _(t):
        st, j, h, p = where_at(t)

        @pl.when(t + AHEAD < 16)
        def _():
            send(t + AHEAD)

        @pl.when(t == 7)
        def _():
            sent_out(1)

        scatter(t)

        @pl.when(j < 2)
        def _():
            for hh in range(2):

                @pl.when(h == hh)
                def _():
                    @pl.when(st == 1)
                    def _():
                        pl.semaphore_wait(free.at[hh], 1)

                    for u in range(SUBS):
                        zback(2 + st, hh, 0, u).start()

        for u in range(SUBS):

            @pl.when(j >= 2)
            def _():
                ring_back(st, j - 2, u)

            piece(SUBS * t + u)
            if u == 1:

                @pl.when(t + AHEAD - 1 < 16)
                def _():
                    forward_back(t + AHEAD - 1)

        @pl.when(t == 9)
        def _():
            finish(0)

        @pl.when((t == 9) | (t == 10) | (t == 12) | (t == 14))
        def _():
            weights((t - 8) // 2)

        @pl.when(t == 9)
        def _():
            dcopy(0).start()

        @pl.when(t >= 10)
        def _():
            s = t - 10
            dcopy(s).wait_recv()
            dacc[s + 2] += dland[s]
            dcopy(s + 1).start()

    wd[0, :, 0:dch] = big[2, rows_at(dp, dch), :].T
    last = [
        pltpu.make_async_copy(big.at[0, rows_at(dp, dch), :], dwg_ref, os_.at[2, 0]),
        pltpu.make_async_copy(big.at[1, rows_at(dp, dch), :], dwu_ref, os_.at[2, 1]),
        pltpu.make_async_copy(wd.at[0, :, pl.ds(0, dch)], dwd_ref, os_.at[3, 0]),
    ]
    for c in last:
        c.start()
    finish(1)
    dcopy(NZ - 2).wait_recv()
    dcomb_ref[...] = dacc[0] + dland[NZ - 2]

    xsent_out(1)
    for h, n in ((0, 4), (1, 3)):
        for s in range(n):
            mcopy(h, s).wait_send()

    @pl.loop(2, 4)
    def _(st):
        for h in range(2):

            @pl.loop(0, NZ - 1)
            def _(s):
                for u in range(SUBS):
                    zback(st, h, s, u).wait_send()

        @pl.loop(0, 8)
        def _(i):
            for k in range(3):
                xback(st, i // 4, i % 4, k, prod).wait_send()
            fback(st, i // 4, i % 4).wait_send()

    @pl.loop(0, NZ - 1)
    def _(s):
        dcopy(s).wait_send()

    @pl.loop(0, 4)
    def _(k):
        ccopy(k).wait_send()

    @pl.loop(0, 9)
    def _(n):
        for i in range(2):
            ycopy(i, n // 3, n % 3).wait_send()

    for c in last:
        c.wait()
    for st in range(2):
        for h in range(2):
            out_copy(st, h).wait()


def layer(tokens, cotangent, routes, combine, w_gate, w_up, w_down, cap):
    n, features = tokens.shape
    ff = w_gate.shape[1]
    hd = features // 2
    per = 2 * cap
    rows = 16 * per
    ft = ff // 3
    ndp = lax.axis_size("dp")
    dch = features // ndp
    ny = ndp // 2
    dma = pltpu.SemaphoreType.DMA
    vmem = pl.BlockSpec(memory_space=pltpu.VMEM)
    hbm = pl.BlockSpec(memory_space=pl.ANY)
    share = jax.ShapeDtypeStruct((dch, ff), BF)
    full = jax.ShapeDtypeStruct((n, features), BF)
    return pl.pallas_call(
        functools.partial(layer_kernel, cap),
        out_shape=(
            full,
            full,
            jax.ShapeDtypeStruct((8, n), F32),
            share,
            share,
            jax.ShapeDtypeStruct((ff, dch), BF),
        ),
        in_specs=[hbm, hbm, vmem, vmem, hbm, hbm, hbm],
        out_specs=(hbm, hbm, vmem, hbm, hbm, hbm),
        scratch_shapes=[
            pltpu.VMEM((2, 2, NZ * n, hd), BF),
            pltpu.VMEM((2, 2, 4, 4 * per, hd), BF),
            pltpu.VMEM((2, 2, rows, hd), BF),
            pltpu.VMEM((4, 2, 4, per, hd), BF),
            pltpu.VMEM((2, 2, 4, 4 * per, hd), BF),
            pltpu.VMEM((2, NZ - 1, n, hd), BF),
            pltpu.VMEM((3, features, ff), BF),
            pltpu.VMEM((2, ff, hd), BF),
            pltpu.VMEM((rows, ft), F32),
            pltpu.VMEM((3, rows, ft), BF),
            pltpu.VMEM((3, rows, ft), BF),
            pltpu.VMEM((3, rows, ft), BF),
            pltpu.VMEM((2, 4, 4 * per, hd), BF),
            pltpu.VMEM((4, 3, dch, ff), BF),
            pltpu.VMEM((2, ny - 1, 3, dch // 2, ff), BF),
            pltpu.VMEM((NZ, 8, n), F32),
            pltpu.VMEM((4, 4 * per, 2 * n), BF),
            pltpu.VMEM((4 * per, 128), F32),
            pltpu.VMEM((4 * per, 2 * n), F32),
            pltpu.VMEM((2, 4, 2 * n, 4 * per), BF),
            pltpu.VMEM((NZ, 8, n), F32),
            pltpu.VMEM((NZ - 1, 8, n), F32),
            dma((4, 2, NZ - 1, SUBS)),
            dma((4, 2, NZ - 1, SUBS)),
            dma((2, 4)),
            dma((2, 4)),
            dma((4, 2, 4, 3)),
            dma((4, 2, 4, 3)),
            dma((4, 2, 4)),
            dma((4, 2, 4)),
            dma((2, 2, 4)),
            dma((8,)),
            dma((4, 2)),
            dma((NZ - 1,)),
            dma((NZ - 1,)),
            dma((4,)),
            dma((4,)),
            dma((2, ny - 1, 3)),
            dma((2, ny - 1, 3)),
            pltpu.SemaphoreType.REGULAR((2,)),
        ],
        compiler_params=pltpu.CompilerParams(
            collective_id=0, has_side_effects=True, vmem_limit_bytes=67043328
        ),
        name="layer",
    )(tokens, cotangent, routes, combine, w_gate, w_up, w_down)


def close_kernel(*refs):
    n = len(refs) // 2
    for src, dst in zip(refs[:n], refs[n:]):
        dst[...] = src[: dst.shape[0]]


def close(arrays, top):
    vmem = pl.BlockSpec(memory_space=pltpu.VMEM)
    shapes = [jax.ShapeDtypeStruct(a.shape, a.dtype) for a in arrays]
    shapes[2] = jax.ShapeDtypeStruct((top, arrays[2].shape[1]), F32)
    return pl.pallas_call(
        close_kernel,
        out_shape=tuple(shapes),
        in_specs=[vmem] * len(arrays),
        out_specs=(vmem,) * len(arrays),
        name="close",
    )(*arrays)


def per_device(tokens, routes, combine, cotangent, w_gate, w_up, w_down):
    n = tokens.shape[0]
    per_token = routes.shape[1]
    experts = w_gate.shape[0] * lax.axis_size("expert")
    cap = 3 * n * per_token // (2 * experts)
    arrays = layer(
        tokens, cotangent, routes.T, combine.T, w_gate[0], w_up[0], w_down[0], cap
    )
    output, d_tokens, d_comb, d_w_gate, d_w_up, d_w_down = close(arrays, per_token)
    return output, d_tokens, d_comb.T, d_w_gate[None], d_w_up[None], d_w_down[None]


def solution(mesh):
    row = P(("dp", "expert"), None)
    weight = P("expert", None, None)
    return jax.shard_map(
        per_device,
        mesh=mesh,
        in_specs=(row, row, row, row, weight, weight, weight),
        out_specs=(
            row,
            row,
            row,
            P("expert", "dp", None),
            P("expert", "dp", None),
            P("expert", None, "dp"),
        ),
        check_vma=False,
    )
```

```python
import functools

import jax
import jax.numpy as jnp
from jax import lax
from jax.experimental import pallas as pl
from jax.experimental.pallas import tpu as pltpu
from jax.sharding import PartitionSpec as P

MESH = pl.DeviceIdType.MESH
NZ = 8
NX = 4
FOUT = 0
LATE = 2
PAIR = 32
RING = 37
AHEAD = 3
SUBS = 4
BF = jnp.bfloat16
F32 = jnp.float32


def neighbours():
    e = lax.axis_index("expert")
    x, z = e // NZ, e % NZ
    zp = x * NZ + (z + 1) % NZ
    zm = x * NZ + (z + NZ - 1) % NZ
    xp = ((x + 1) % NX) * NZ + z
    xm = ((x + NX - 1) % NX) * NZ + z
    return x, z, zp, zm, xp, xm


def rcopy(src, dst, send, recv, dev):
    return pltpu.make_async_remote_copy(
        src_ref=src,
        dst_ref=dst,
        send_sem=send,
        recv_sem=recv,
        device_id={"expert": dev},
        device_id_type=MESH,
    )


def row_masks(meta, x, z, cap, blk):
    width = meta.shape[1]
    per = 2 * cap
    col = lax.broadcasted_iota(jnp.int32, (per, width), 1)
    row = lax.broadcasted_iota(jnp.int32, (per, width), 0)
    second = (row >= cap).astype(jnp.int32)
    shift = (col[0:1] >= width // 2).astype(jnp.int32) * 4096
    expert = ((x + blk + 1) % NX) * NZ + z
    ids = row - cap * second + 4096 * second + expert * cap
    return [ids == (meta[k : k + 1, :].astype(jnp.int32) + shift) for k in range(4)]


def layer_kernel(
    cap,
    tok_ref,
    cot_ref,
    routes_ref,
    combine_ref,
    wg_ref,
    wu_ref,
    wd_ref,
    out_ref,
    dtok_ref,
    dcomb_ref,
    dwg_ref,
    dwu_ref,
    dwd_ref,
    ag,
    sx,
    r,
    relay,
    q,
    land,
    big,
    wd,
    gate,
    hid,
    dga,
    act,
    prod,
    lc,
    ly,
    metab,
    smat,
    cmat,
    smatf,
    stmat,
    dacc,
    dland,
    zs,
    zr,
    ms,
    mr,
    xs,
    xr,
    rs,
    rr,
    ls,
    ws,
    os_,
    ds_,
    dr,
    cs,
    cr,
    ys,
    yr,
    free,
):
    tokens, features = tok_ref.shape
    ff = wg_ref.shape[1]
    hd = features // 2
    per = 2 * cap
    sub = tokens // SUBS
    ft, nt = ff // 3, features // 4
    x, z, zp, zm, xp, xm = neighbours()
    zdev = (zp, zm)
    dp = lax.axis_index("dp")
    y, core = dp // 2, dp % 2
    chunks = lax.axis_size("dp")
    ny = chunks // 2
    dch = features // chunks
    half = dch // 2
    ydev = (((y + 1) % ny) * 2 + core, ((y + ny - 1) % ny) * 2 + core)
    partner = 2 * y + 1 - core

    def rows_at(n, size):
        return pl.ds(pl.multiple_of(n * size, size), size)

    loads = [
        (tok_ref.at[:, pl.ds(0, hd)], ag.at[0, 0, pl.ds(0, tokens), :]),
        (tok_ref.at[:, pl.ds(hd, hd)], ag.at[0, 1, pl.ds(0, tokens), :]),
        (cot_ref.at[:, pl.ds(0, hd)], ag.at[1, 0, pl.ds(0, tokens), :]),
        (cot_ref.at[:, pl.ds(hd, hd)], ag.at[1, 1, pl.ds(0, tokens), :]),
        (wg_ref, big.at[0]),
        (wu_ref, big.at[1]),
        (wd_ref.at[:, pl.ds(0, hd)], wd.at[0]),
        (wd_ref.at[:, pl.ds(hd, hd)], wd.at[1]),
    ]

    def load(i):
        return pltpu.make_async_copy(*loads[i], ws.at[i])

    for i in range(4):
        load(i).start()

    barrier = pltpu.get_barrier_semaphore()
    for d in (zp, zm, xp, xm):
        pl.semaphore_signal(barrier, inc=1, device_id={"expert": d}, device_id_type=MESH)
    for d in (partner, *ydev):
        pl.semaphore_signal(barrier, inc=1, device_id={"dp": d}, device_id_type=MESH)
    pl.semaphore_wait(barrier, 7)

    def where_at(t):
        st, j = t // 8, t % 8
        h = j % 2
        return st, j, h, jnp.where(h == 0, j // 2, 3 - j // 2)


    def zout(st, h, s, u):
        a = s if h == 0 else (NZ - s) % NZ
        b = s + 1 if h == 0 else NZ - 1 - s
        src = ag.at[st, h, pl.ds(pl.multiple_of(a * tokens + sub * u, sub), sub), :]
        dst = ag.at[st, h, pl.ds(pl.multiple_of(b * tokens + sub * u, sub), sub), :]
        return rcopy(src, dst, zs.at[st, h, s, u], zr.at[st, h, s, u], zdev[h])

    def mcopy(h, s):
        a = s if h == 0 else (NZ - s) % NZ
        b = s + 1 if h == 0 else NZ - 1 - s
        return rcopy(metab.at[a], metab.at[b], ms.at[h, s], mr.at[h, s], zdev[h])

    def xout(st, h, p, i):
        far = jnp.where(h == 0, xp, xm)
        dst = relay.at[st, h, p] if i == 0 else r.at[st, h, rows_at(p * 4 + i - 1, per), :]
        return rcopy(
            sx.at[st, h, p, pl.ds((1, 0, 2)[i] * per, per), :],
            dst,
            xs.at[st, h, p, i],
            xr.at[st, h, p, i],
            (far, xp, xm)[i],
        )

    def fout(st, h, p):
        far = jnp.where(h == 0, xp, xm)
        return rcopy(
            relay.at[st, h, p],
            r.at[st, h, rows_at(p * 4 + 2, per), :],
            rs.at[st, h, p],
            rr.at[st, h, p],
            far,
        )


    def xback(st, h, p, i, src):
        far = jnp.where(h == 0, xp, xm)
        dst = relay.at[st, h, p] if i == 0 else q.at[st - 2, h, p, pl.ds((0, 2)[i - 1] * per, per), :]
        return rcopy(
            src.at[h, p, pl.ds((2, 0, 1)[i] * per, per), :],
            dst,
            xs.at[st, h, p, i],
            xr.at[st, h, p, i],
            (far, xm, xp)[i],
        )

    def fback(st, h, p):
        far = jnp.where(h == 0, xp, xm)
        return rcopy(
            relay.at[st, h, p],
            q.at[st - 2, h, p, pl.ds(per, per), :],
            rs.at[st, h, p],
            rr.at[st, h, p],
            far,
        )

    drow = sx.at[0]
    srcs = (prod, drow)

    def own(st, h, p, src):
        return pltpu.make_async_copy(
            src.at[h, p, pl.ds(3 * per, per), :],
            q.at[st - 2, h, p, pl.ds(3 * per, per), :],
            ls.at[st - 2, h, p],
        )

    def chunk(h, s):
        return s + 1 if h == 0 else NZ - 1 - s

    def zback(st, h, s, u):
        m = chunk(h, s)
        src = ag.at[st - 2, h, pl.ds(pl.multiple_of(m * tokens + sub * u, sub), sub), :]
        dst = land.at[h, s, pl.ds(sub * u, sub), :]
        return rcopy(src, dst, zs.at[st, h, s, u], zr.at[st, h, s, u], zdev[h])

    def dcopy(s):
        return rcopy(dacc.at[s + 1], dland.at[s], ds_.at[s], dr.at[s], zp)


    def dpcopy(src, dst, send, recv, dev):
        return pltpu.make_async_remote_copy(
            src_ref=src,
            dst_ref=dst,
            send_sem=send,
            recv_sem=recv,
            device_id={"dp": dev},
            device_id_type=MESH,
        )

    def target(k):
        return (y + jnp.where(k == 0, ny - 1, jnp.where(k == 3, 0, k))) % ny

    def ccopy(k):
        src = big.at[:, rows_at(2 * target(k) + 1 - core, dch), :]
        return dpcopy(src, lc.at[k], cs.at[k], cr.at[k], partner)

    def ycopy(i, s, g):
        a = (y + 2 * ny - 1 - s) % ny if i == 0 else (y + 1 + s) % ny
        src = big.at[g, rows_at(2 * (2 * a + core) + i, half), :]
        return dpcopy(src, ly.at[i, s, g], ys.at[i, s, g], yr.at[i, s, g], ydev[i])


    for h in range(2):
        load(h).wait()
        for u in range(SUBS):
            zout(0, h, 0, u).start()
    for i in range(4, 8):
        load(i).start()

    experts = NX * NZ
    names = [routes_ref[k : k + 1, :] for k in range(4)]
    ids = lax.broadcasted_iota(jnp.int32, (experts, tokens), 0)
    hits = [ids == n for n in names]
    count = sum(hit.astype(F32) for hit in hits)
    earlier = lax.broadcasted_iota(jnp.int32, (tokens, tokens), 0)
    later = lax.broadcasted_iota(jnp.int32, (tokens, tokens), 1)
    before = jnp.dot(
        count.astype(BF), (earlier < later).astype(F32).astype(BF), preferred_element_type=F32
    )
    for k in range(4):
        slot = jnp.sum(jnp.where(hits[k], before, 0.0), axis=0, keepdims=True)
        metab[0, k : k + 1, :] = names[k].astype(F32) * cap + slot
        metab[0, 4 + k : 5 + k, :] = combine_ref[k : k + 1, :]
    for h in range(2):
        mcopy(h, 0).start()
    for i in range(2, 4):
        load(i).wait()

    cmat[...] = jnp.zeros_like(cmat)

    def meta_of(p):
        return jnp.concatenate([metab[2 * p], metab[2 * p + 1]], axis=1)

    def masks(p):
        meta = meta_of(p)
        for blk in range(NX):
            at = pl.ds(blk * per, per)
            hit = row_masks(meta, x, z, cap, blk)
            one = functools.reduce(jnp.logical_or, hit).astype(F32)
            weight = sum(jnp.where(hit[k], meta[4 + k : 5 + k, :], 0.0) for k in range(4))
            smatf[at, :] = weight
            smat[p, at, :] = one.astype(BF)
            here = lax.broadcasted_iota(jnp.int32, (per, 128), 1) == p
            cmat[at, :] = jnp.where(here, jnp.sum(weight, axis=1, keepdims=True), cmat[at, :])
        stmat[0, p] = smatf[...].T.astype(BF)
        stmat[1, p] = smat[p].T

    def row_weights(p, at):
        size = cmat.shape[0] if at is None else per
        here = lax.broadcasted_iota(jnp.int32, (size, 128), 1) == p
        return jnp.sum(jnp.where(here, cmat[...] if at is None else cmat[at, :], 0.0), axis=1, keepdims=True)

    def forward_out(t):
        st, _, h, p = where_at(t)
        xout(st, h, p, 0).wait_recv()
        fout(st, h, p).start()

    def arrived(st):
        @pl.loop(0, 8)
        def _(i):
            h, p = i // 4, i % 4
            for k in (1, 2):
                xout(st, h, p, k).wait_recv()
            fout(st, h, p).wait_recv()

    def ring_out(t, u):
        st, j, _, _ = where_at(t)

        @pl.when(j < NZ - 1)
        def _():
            for h in range(2):
                zout(st, h, j, u).wait_recv()

                @pl.when(j < NZ - 2)
                def _():
                    zout(st, h, j + 1, u).start()

                @pl.when((j == NZ - 2) & (st == 0))
                def _():
                    zout(1, h, 0, u).start()

    def project(i, f):
        lanes = rows_at(f, ft)
        a = jnp.dot(r[0, 0], big[i, 0:hd, lanes], preferred_element_type=F32)
        return a + jnp.dot(r[0, 1], big[i, hd:, lanes], preferred_element_type=F32)

    def gate_tile(f):
        gate[...] = project(0, f)

    def up_tile(f):
        up = project(1, f)
        g = gate[...]
        sig = 1.0 / (1.0 + jnp.exp(-g))
        a = g * sig
        act[f] = a.astype(BF)
        hid[f] = (a * up).astype(BF)
        dga[f] = (up * sig * (1.0 + g * (1.0 - sig))).astype(BF)

    def down_tile(n):
        lanes = pl.ds((n % 2) * nt, nt)
        out = sum(
            jnp.dot(hid[f], wd[n // 2, f * ft : (f + 1) * ft, lanes], preferred_element_type=F32)
            for f in range(3)
        )
        prod[n // 2, :, :, lanes] = out.astype(BF).reshape(4, 4 * per, nt)

    def send(t):
        st, _, h, p = where_at(t)
        for i in range(2):

            @pl.when(st == i)
            def _():
                for k in range(3):
                    xback(2 + i, h, p, k, srcs[i]).start()
                own(2 + i, h, p, srcs[i]).start()

    def forward_back(t):
        st, _, h, p = where_at(t)
        xback(2 + st, h, p, 0, prod).wait_recv()
        fback(2 + st, h, p).start()

    @pl.loop(0, 16)
    def _(t):
        st, j, h, p = where_at(t)

        @pl.when(st == 0)
        def _():
            for hh, n in ((0, 4), (1, 3)):

                @pl.when(j < n)
                def _():
                    mcopy(hh, j).wait_recv()

                @pl.when(j + 1 < n)
                def _():
                    mcopy(hh, j + 1).start()

        for u in range(SUBS):
            ring_out(t, u)
            if u == 0:

                @pl.when(t == 10)
                def _():
                    arrived(0)
                    for i in range(4, 8):
                        load(i).wait()

            slot = SUBS * (t - 10) + u

            @pl.when((slot >= 0) & (slot < 6))
            def _():
                if u % 2 == 0:
                    gate_tile(slot // 2)
                else:
                    up_tile(slot // 2)

            for i in range(4):
                if (6 + i) % SUBS == u:

                    @pl.when(slot == 6 + i)
                    def _():
                        down_tile(i)

            if u == FOUT:

                @pl.when(t >= LATE)
                def _():
                    forward_out(t - LATE)

            if u == 2:
                for i in range(3):

                    @pl.when(t == 12 + i)
                    def _():
                        send(i)

            if u == 3:
                for i in range(2):

                    @pl.when(t == 14 + i)
                    def _():
                        forward_back(i)

        @pl.when(t < 4)
        def _():
            masks(p)

        got = jnp.dot(
            smat[p], ag[st, h, rows_at(p, 2 * tokens), :], preferred_element_type=F32
        )
        got = (got * jnp.where(st == 1, row_weights(p, None), 1.0)).astype(BF)
        sx[st, h, p] = got
        r[st, h, rows_at(p * 4 + 3, per), :] = got[3 * per :]
        for i in range(3):
            xout(st, h, p, i).start()

    forward_out(14)

    def sent_out(st):
        for h in range(2):

            @pl.loop(0, NZ - 1)
            def _(s):
                for u in range(SUBS):
                    zout(st, h, s, u).wait_send()

    def xsent_out(st):
        @pl.loop(0, 8)
        def _(i):
            for k in range(3):
                xout(st, i // 4, i % 4, k).wait_send()
            fout(st, i // 4, i % 4).wait_send()

    sent_out(0)

    def scatter(t):
        st, _, h, p = where_at(t)
        for k in (1, 2):
            xback(2 + st, h, p, k, prod).wait_recv()
        fback(2 + st, h, p).wait_recv()
        own(2 + st, h, p, prod).wait()
        ag[st, h, rows_at(p, 2 * tokens), :] = jnp.dot(
            stmat[st, p], q[st, h, p], preferred_element_type=F32
        ).astype(BF)

    def upstream(h):
        return {"expert": zm if h == 0 else zp}

    def give_slot(h):
        pl.semaphore_signal(free.at[h], inc=1, device_id=upstream(h), device_id_type=MESH)

    def ring_back(st, s, u):
        for h in range(2):
            at = pl.ds(pl.multiple_of(chunk(h, s + 1) * tokens + sub * u, sub), sub)
            zback(2 + st, h, s, u).wait_recv()
            ag[st, h, at, :] += land[h, s, pl.ds(sub * u, sub), :]
            if u == 0:

                @pl.when(st == 1)
                def _():
                    pl.semaphore_wait(free.at[h], 1)

            zback(2 + st, h, s + 1, u).start()
            if u == SUBS - 1:

                @pl.when(st == 0)
                def _():
                    give_slot(h)

    def out_copy(st, h):
        return pltpu.make_async_copy(
            ag.at[st, h, pl.ds(0, tokens), :],
            (out_ref, dtok_ref)[st].at[:, pl.ds(h * hd, hd)],
            os_.at[st, h],
        )

    def finish(st):
        for h in range(2):
            for u in range(SUBS):
                zback(2 + st, h, NZ - 2, u).wait_recv()
            ag[st, h, 0:tokens, :] += land[h, NZ - 2]
            if st == 0:
                give_slot(h)
            out_copy(st, h).start()

    def weights(p):
        meta = meta_of(p)
        total = [jnp.zeros((1, 2 * tokens), F32)] * 4
        for blk in range(NX):
            at = pl.ds(blk * per, per)
            v = jnp.zeros((per, 1), F32)
            for h in range(2):
                v = v + jnp.sum(
                    q[0, h, p, at, :].astype(F32) * sx[1, h, p, at, :].astype(F32),
                    axis=1,
                    keepdims=True,
                )
            hit = row_masks(meta, x, z, cap, blk)
            c = row_weights(p, at)
            v = v / jnp.where(c > 0.0, c, 1.0)
            for k in range(4):
                total[k] = total[k] + jnp.sum(jnp.where(hit[k], v, 0.0), axis=0, keepdims=True)
        for i in range(2):
            for k in range(4):
                dacc[2 * p + i, k : k + 1, :] = total[k][:, i * tokens : (i + 1) * tokens]
            dacc[2 * p + i, 4:8, :] = jnp.zeros((4, tokens), F32)

    def nt_dot(a, b):
        return lax.dot_general(a, b, (((1,), (1,)), ((), ())), preferred_element_type=F32)

    def hidden_first(f):
        gate[...] = nt_dot(r[1, 0], wd[0, rows_at(f, ft), :])

    def hidden_second(f):
        dh = gate[...] + nt_dot(r[1, 1], wd[1, rows_at(f, ft), :])
        dga[f] = (dh * dga[f].astype(F32)).astype(BF)
        act[f] = (dh * act[f].astype(F32)).astype(BF)

    def row_tile(n):
        at = rows_at(n, dch)
        out = sum(
            nt_dot(dga[f], big[0, at, f * ft : (f + 1) * ft])
            + nt_dot(act[f], big[1, at, f * ft : (f + 1) * ft])
            for f in range(3)
        )
        each = chunks // 2
        sx[0, n // each, :, :, rows_at(n % each, dch)] = out.astype(BF).reshape(4, 4 * per, dch)

    def grad_chunk(c):
        each = chunks // 2
        lanes = rows_at(c % each, dch)
        a = r[0, c // each, :, lanes].T
        b = r[1, c // each, :, lanes].T
        for i, (lhs, rhs) in enumerate(((a, dga), (a, act), (b, hid))):
            for f in range(3):
                big[i, rows_at(c, dch), f * ft : (f + 1) * ft] = jnp.dot(
                    lhs, rhs[f], preferred_element_type=F32
                ).astype(BF)

    def grad_piece(k):
        kk = k % 4
        grad_chunk(2 * target(kk) + jnp.where(k >= 4, core, 1 - core))

        @pl.when(k < 4)
        def _():
            ccopy(kk).start()

    def pair_sum(k):
        at = rows_at(2 * target(k) + core, dch)
        ccopy(k).wait_recv()
        for i in range(3):
            big[i, at, :] += lc[k, i]

        for i in range(2):

            @pl.when(k == i)
            def _():
                for g in range(3):
                    ycopy(i, 0, g).start()

    def dp_ring(n):
        s, g = n // 3, n % 3
        for i in range(2):
            b = (y + 2 * ny - 2 - s) % ny if i == 0 else (y + 2 + s) % ny
            ycopy(i, s, g).wait_recv()
            big[g, rows_at(2 * (2 * b + core) + i, half), :] += ly[i, s, g]

            @pl.when(s < ny - 2)
            def _():
                ycopy(i, s + 1, g).start()

    def piece(slot):
        @pl.when(slot == 10)
        def _():
            arrived(1)

        @pl.when((slot >= 10) & (slot < 16))
        def _():
            @pl.when(slot % 2 == 0)
            def _():
                hidden_first((slot - 10) // 2)

            @pl.when(slot % 2 == 1)
            def _():
                hidden_second((slot - 10) // 2)

        @pl.when((slot >= 16) & (slot < 16 + chunks))
        def _():
            row_tile(slot - 16)

        @pl.when((slot >= 24) & (slot < 32))
        def _():
            grad_piece(slot - 24)

        @pl.when((slot >= PAIR) & (slot < PAIR + 4))
        def _():
            pair_sum(slot - PAIR)

        @pl.when((slot >= RING) & (slot < RING + 27) & ((slot - RING) % 3 == 0))
        def _():
            dp_ring((slot - RING) // 3)

    @pl.loop(0, 16)
    def _(t):
        st, j, h, p = where_at(t)

        @pl.when(t + AHEAD < 16)
        def _():
            send(t + AHEAD)

        @pl.when(t == 7)
        def _():
            sent_out(1)

        scatter(t)

        @pl.when(j < 2)
        def _():
            for hh in range(2):

                @pl.when(h == hh)
                def _():
                    @pl.when(st == 1)
                    def _():
                        pl.semaphore_wait(free.at[hh], 1)

                    for u in range(SUBS):
                        zback(2 + st, hh, 0, u).start()

        for u in range(SUBS):

            @pl.when(j >= 2)
            def _():
                ring_back(st, j - 2, u)

            piece(SUBS * t + u)
            if u == 0:

                @pl.when(t == 0)
                def _():
                    forward_back(2)

            if u == 1:

                @pl.when(t == 0)
                def _():
                    forward_out(15)
                    xsent_out(0)

                @pl.when((t >= 1) & (t + 2 < 16))
                def _():
                    forward_back(t + 2)

        @pl.when(t == 9)
        def _():
            finish(0)

        @pl.when((t == 9) | (t == 10) | (t == 12) | (t == 14))
        def _():
            weights((t - 8) // 2)

        @pl.when(t == 9)
        def _():
            dcopy(0).start()

        @pl.when(t >= 10)
        def _():
            s = t - 10
            dcopy(s).wait_recv()
            dacc[s + 2] += dland[s]
            dcopy(s + 1).start()

    wd[0, :, 0:dch] = big[2, rows_at(dp, dch), :].T
    last = [
        pltpu.make_async_copy(big.at[0, rows_at(dp, dch), :], dwg_ref, os_.at[2, 0]),
        pltpu.make_async_copy(big.at[1, rows_at(dp, dch), :], dwu_ref, os_.at[2, 1]),
        pltpu.make_async_copy(wd.at[0, :, pl.ds(0, dch)], dwd_ref, os_.at[3, 0]),
    ]
    for c in last:
        c.start()
    finish(1)
    dcopy(NZ - 2).wait_recv()
    dcomb_ref[...] = dacc[0] + dland[NZ - 2]

    xsent_out(1)
    for h, n in ((0, 4), (1, 3)):
        for s in range(n):
            mcopy(h, s).wait_send()

    @pl.loop(2, 4)
    def _(st):
        for h in range(2):

            @pl.loop(0, NZ - 1)
            def _(s):
                for u in range(SUBS):
                    zback(st, h, s, u).wait_send()

        @pl.loop(0, 8)
        def _(i):
            for k in range(3):
                xback(st, i // 4, i % 4, k, prod).wait_send()
            fback(st, i // 4, i % 4).wait_send()

    @pl.loop(0, NZ - 1)
    def _(s):
        dcopy(s).wait_send()

    @pl.loop(0, 4)
    def _(k):
        ccopy(k).wait_send()

    @pl.loop(0, 9)
    def _(n):
        for i in range(2):
            ycopy(i, n // 3, n % 3).wait_send()

    for c in last:
        c.wait()
    for st in range(2):
        for h in range(2):
            out_copy(st, h).wait()


def layer(tokens, cotangent, routes, combine, w_gate, w_up, w_down, cap):
    n, features = tokens.shape
    ff = w_gate.shape[1]
    hd = features // 2
    per = 2 * cap
    rows = 16 * per
    ft = ff // 3
    ndp = lax.axis_size("dp")
    dch = features // ndp
    ny = ndp // 2
    dma = pltpu.SemaphoreType.DMA
    vmem = pl.BlockSpec(memory_space=pltpu.VMEM)
    hbm = pl.BlockSpec(memory_space=pl.ANY)
    share = jax.ShapeDtypeStruct((dch, ff), BF)
    full = jax.ShapeDtypeStruct((n, features), BF)
    return pl.pallas_call(
        functools.partial(layer_kernel, cap),
        out_shape=(
            full,
            full,
            jax.ShapeDtypeStruct((8, n), F32),
            share,
            share,
            jax.ShapeDtypeStruct((ff, dch), BF),
        ),
        in_specs=[hbm, hbm, vmem, vmem, hbm, hbm, hbm],
        out_specs=(hbm, hbm, vmem, hbm, hbm, hbm),
        scratch_shapes=[
            pltpu.VMEM((2, 2, NZ * n, hd), BF),
            pltpu.VMEM((2, 2, 4, 4 * per, hd), BF),
            pltpu.VMEM((2, 2, rows, hd), BF),
            pltpu.VMEM((4, 2, 4, per, hd), BF),
            pltpu.VMEM((2, 2, 4, 4 * per, hd), BF),
            pltpu.VMEM((2, NZ - 1, n, hd), BF),
            pltpu.VMEM((3, features, ff), BF),
            pltpu.VMEM((2, ff, hd), BF),
            pltpu.VMEM((rows, ft), F32),
            pltpu.VMEM((3, rows, ft), BF),
            pltpu.VMEM((3, rows, ft), BF),
            pltpu.VMEM((3, rows, ft), BF),
            pltpu.VMEM((2, 4, 4 * per, hd), BF),
            pltpu.VMEM((4, 3, dch, ff), BF),
            pltpu.VMEM((2, ny - 1, 3, dch // 2, ff), BF),
            pltpu.VMEM((NZ, 8, n), F32),
            pltpu.VMEM((4, 4 * per, 2 * n), BF),
            pltpu.VMEM((4 * per, 128), F32),
            pltpu.VMEM((4 * per, 2 * n), F32),
            pltpu.VMEM((2, 4, 2 * n, 4 * per), BF),
            pltpu.VMEM((NZ, 8, n), F32),
            pltpu.VMEM((NZ - 1, 8, n), F32),
            dma((4, 2, NZ - 1, SUBS)),
            dma((4, 2, NZ - 1, SUBS)),
            dma((2, 4)),
            dma((2, 4)),
            dma((4, 2, 4, 3)),
            dma((4, 2, 4, 3)),
            dma((4, 2, 4)),
            dma((4, 2, 4)),
            dma((2, 2, 4)),
            dma((8,)),
            dma((4, 2)),
            dma((NZ - 1,)),
            dma((NZ - 1,)),
            dma((4,)),
            dma((4,)),
            dma((2, ny - 1, 3)),
            dma((2, ny - 1, 3)),
            pltpu.SemaphoreType.REGULAR((2,)),
        ],
        compiler_params=pltpu.CompilerParams(
            collective_id=0, has_side_effects=True, vmem_limit_bytes=67043328
        ),
        name="layer",
    )(tokens, cotangent, routes, combine, w_gate, w_up, w_down)


def close_kernel(*refs):
    n = len(refs) // 2
    for src, dst in zip(refs[:n], refs[n:]):
        dst[...] = src[: dst.shape[0]]


def close(arrays, top):
    vmem = pl.BlockSpec(memory_space=pltpu.VMEM)
    shapes = [jax.ShapeDtypeStruct(a.shape, a.dtype) for a in arrays]
    shapes[2] = jax.ShapeDtypeStruct((top, arrays[2].shape[1]), F32)
    return pl.pallas_call(
        close_kernel,
        out_shape=tuple(shapes),
        in_specs=[vmem] * len(arrays),
        out_specs=(vmem,) * len(arrays),
        name="close",
    )(*arrays)


def per_device(tokens, routes, combine, cotangent, w_gate, w_up, w_down):
    n = tokens.shape[0]
    per_token = routes.shape[1]
    experts = w_gate.shape[0] * lax.axis_size("expert")
    cap = 3 * n * per_token // (2 * experts)
    arrays = layer(
        tokens, cotangent, routes.T, combine.T, w_gate[0], w_up[0], w_down[0], cap
    )
    output, d_tokens, d_comb, d_w_gate, d_w_up, d_w_down = close(arrays, per_token)
    return output, d_tokens, d_comb.T, d_w_gate[None], d_w_up[None], d_w_down[None]


def solution(mesh):
    row = P(("dp", "expert"), None)
    weight = P("expert", None, None)
    return jax.shard_map(
        per_device,
        mesh=mesh,
        in_specs=(row, row, row, row, weight, weight, weight),
        out_specs=(
            row,
            row,
            row,
            P("expert", "dp", None),
            P("expert", "dp", None),
            P("expert", None, "dp"),
        ),
        check_vma=False,
    )
```
